32 devices in a mesh: row: 8 (over y, x, core), col: 4 (over z).
Axes of the slice: x: 2, y: 2, z: 4, core: 2. Of those that a mesh axis runs over, the one named last changes fastest.
Arguments:
- density: bfloat16 [32, 5, 256, 256], P('row', None, 'col'), may hold values from -1 to 2, as said below
- pattern: int32 [32, 5], P('row'), may hold values from 0 to 1, as said below
- windows: int32 [64], P(('row', 'col')), may hold values from 0 to 61, as said below
- basis_values: bfloat16 [64, 4096, 384], P(('row', 'col')), may hold values from -6 to 6
- basis_grads: bfloat16 [3, 64, 4096, 384], P(None, ('row', 'col')), may hold values from -48 to 48
- weights: float32 [64, 4096], P(('row', 'col')), may hold values from 0.25 to 4
Outputs:
- purified: bfloat16 [32, 5, 256, 256], P('row', None, 'col')
- xc_matrix: float32 [32, 5, 256, 256], P('row', None, 'col')
- grid_density: float32 [64, 4096], P(('row', 'col'))
The draws below stay inside these ranges and needn't reach their ends.
Inputs may be any that keep to these rules, and one draw needn't show every extreme that they name: density[i, d] is block (i, i + d - 2) of a symmetric matrix: density[i, d] equals density[i + d - 2, 4 - d] transposed; blocks whose column block lies outside the matrix are 0. pattern[i, d] = pattern[i + d - 2, 4 - d]; it is 1 for d = 1, 2, 3 where block i + d - 2 exists and 0 where it does not. Tile t lies on device t // 2 of the joined axes row+col; if that device has row index q, windows[t] lies between 2 * 4 q - 2 and 2 * 4 q + 2 * 4 - 1.
All inputs are finite; a program needn't handle non-finite values.
Results may differ from the reference program's by a relative error of at most 0.011.
Values may be sent and summed in bfloat16 or wider, within the bound.
No kernel may reach another device: no remote copies, remote signals or barrier semaphores. Data moves between devices by JAX's collectives and lax.ppermute only.
A program may use at most 128 MiB of HBM per device.

```python
import math
import jax
import jax.numpy as jnp
from jax import lax

BS = 256
HB = 128
FN = 384
BD = 4
BLOCKS = 32
TILES_DEV = 2
POINTS = 4096
NTILES = 64
ITERS = 2
N_COL = 4


def draw_density(key, part):
    noise_key = jax.random.fold_in(key, 11)
    diag_key = jax.random.fold_in(key, 12)
    noise = jnp.clip(jax.random.normal(noise_key, (BLOCKS, 5, BS, BS), jnp.float32), -4.0, 4.0)
    level = 0.6
    diagonal = jax.random.uniform(diag_key, (BLOCKS, BS), jnp.float32, 0.2, 0.8)
    padded = jnp.pad(noise, ((2, 2), (0, 0), (0, 0), (0, 0)))
    partners = jnp.stack([jnp.swapaxes(padded[band:band + BLOCKS, 4 - band], 1, 2) for band in range(5)], axis=1)
    symmetric = (noise + partners) * (0.5 * level / jnp.sqrt(jnp.float32(5 * BS)))
    block_ids = jnp.arange(BLOCKS, dtype=jnp.int32)[:, None]
    band_ids = jnp.arange(5, dtype=jnp.int32)[None, :]
    partner_ids = block_ids + band_ids - 2
    valid = ((partner_ids >= 0) & (partner_ids < BLOCKS))[:, :, None, None]
    identity = jnp.eye(BS, dtype=jnp.float32)[None, None]
    centre = (band_ids == 2)[:, :, None, None]
    filled = jnp.where(centre, symmetric * (1.0 - identity) + identity * diagonal[:, None, None, :], symmetric)
    return jnp.where(valid, filled, 0.0).astype(jnp.bfloat16)


def draw_pattern(key, part):
    picks = jax.random.randint(jax.random.fold_in(key, 21), (BLOCKS,), 0, 2)
    block_ids = jnp.arange(BLOCKS, dtype=jnp.int32)[:, None]
    band_ids = jnp.arange(5, dtype=jnp.int32)[None, :]
    partner_ids = block_ids + band_ids - 2
    valid = (partner_ids >= 0) & (partner_ids < BLOCKS)
    earlier = jnp.roll(picks, 2)[:, None]
    far = jnp.where(band_ids == 4, picks[:, None], jnp.where(band_ids == 0, earlier, 0))
    near = jnp.abs(band_ids - 2) <= 1
    return jnp.where(valid, jnp.where(near, 1, far), 0).astype(jnp.int32)


def draw_windows(key, part):
    tiles_idx = jnp.arange(NTILES, dtype=jnp.int32)
    row_of = tiles_idx // TILES_DEV // N_COL
    lowest = jnp.maximum(0, 2 * BD * row_of - 2)
    highest = jnp.minimum(2 * BLOCKS - 3, 2 * BD * row_of + 2 * BD - 1)
    picks = jax.random.randint(jax.random.fold_in(key, 31), (NTILES,), 0, 1 << 20)
    return (lowest + picks % (highest - lowest + 1)).astype(jnp.int32)


def steps_of(key, shape, cuts, least, high):
    level = 1.0
    for dim, blocks in cuts:
        heights = jax.random.uniform(jax.random.fold_in(jax.random.fold_in(key, 6), dim), (blocks,), jnp.float32, least / len(cuts), high / len(cuts))
        level = level * jnp.repeat(jnp.exp(heights), shape[dim] // blocks).reshape((-1,) + (1,) * (len(shape) - 1 - dim))
    return level


def gaussian(key, dims, scale, most, shards=(), held_as=jnp.bfloat16):
    values = scale * jax.random.normal(key, dims, jnp.float32)
    if shards:
        values = values * steps_of(key, dims, shards, -0.22, 0.18)
    return jnp.clip(values, -most, most).astype(held_as)


def setup_inputs(seed: int = 0) -> dict:
    key_list = jax.random.split(jax.random.key(seed), 7)
    density = draw_density(jax.random.fold_in(key_list[6], 71), 0)
    pattern = draw_pattern(jax.random.fold_in(key_list[6], 71), 0)
    windows = draw_windows(jax.random.fold_in(key_list[6], 71), 0)
    basis_values = gaussian(key_list[3], (NTILES, POINTS, FN), 1.0, 6.0, ((0, 32),))
    basis_grads = gaussian(key_list[4], (3, NTILES, POINTS, FN), 8.0, 48.0, ((1, 32),))
    weights = jnp.clip(jnp.exp(math.log(4.0) - 2.7725887 * jax.random.uniform(key_list[5], (NTILES, POINTS), jnp.float32) ** steps_of(key_list[5], (NTILES, POINTS), ((0, 32),), -0.2, 0.2)), 0.25, 4.0)
    return dict(density=density, pattern=pattern, windows=windows, basis_values=basis_values, basis_grads=basis_grads, weights=weights)


slater_cx = 0.7386
kappa_pbe = 0.804
mu_pbe = 0.2195

def energy_sum(point_density, grad_square):
    spread = jnp.sqrt(point_density * point_density + 1.0)
    reduced = grad_square / spread ** (8.0 / 3.0)
    enhance = 1.0 + kappa_pbe - kappa_pbe / (1.0 + mu_pbe * reduced / kappa_pbe)
    return jnp.sum(-slater_cx * spread ** (4.0 / 3.0) * enhance)

def tile_terms(values, grads, quadrature, window_block):
    functions = values.shape[1]
    points = values.shape[0]
    projected = jnp.dot(values, window_block, preferred_element_type=jnp.float32)
    point_density = lax.optimization_barrier(jnp.sum(projected * values.astype(jnp.float32), axis=1)) / functions
    slopes = 2.0 * lax.optimization_barrier(jnp.sum(projected[None] * grads.astype(jnp.float32), axis=2)) / functions
    grad_square = lax.optimization_barrier(jnp.sum(slopes * slopes, axis=0))
    by_density, by_gradient = jax.grad(energy_sum, argnums=(0, 1))(point_density, grad_square)
    scaled = quadrature / points
    weighted = (0.5 * by_density * scaled)[:, None] * values.astype(jnp.float32)
    weighted = weighted + lax.optimization_barrier(jnp.sum(((2.0 * by_gradient * scaled)[None] * slopes)[:, :, None] * grads.astype(jnp.float32), axis=0))
    weighted = weighted.astype(jnp.bfloat16)
    one_side = lax.dot_general(values, weighted, (((0,), (0,)), ((), ())), preferred_element_type=jnp.float32)
    return (point_density, one_side + one_side.T)

def band_product(left, right_padded):
    blocks = left.shape[0]
    total = None
    for offset_step in range(5):
        shifted = right_padded[offset_step:offset_step + blocks]
        widened = jnp.pad(shifted, ((0, 0), (2, 2), (0, 0), (0, 0)))
        picked = widened[:, 4 - offset_step:9 - offset_step]
        term = jnp.einsum('brk,bdkc->bdrc', left[:, offset_step].astype(jnp.float32), picked.astype(jnp.float32))
        total = term if total is None else total + term
    return total

def window_of(band_three, lead, offset, functions):
    paired = lax.dynamic_slice_in_dim(band_three, lead, 2, 0)
    upper = jnp.concatenate([paired[0, 1], paired[0, 2]], axis=1)
    lower = jnp.concatenate([paired[1, 0], paired[1, 1]], axis=1)
    dense = jnp.concatenate([upper, lower], axis=0)
    return lax.dynamic_slice(dense, (offset, offset), (functions, functions))

def spread_term(summed, term, lead, offset):
    width = summed.shape[2]
    dense = lax.dynamic_update_slice(jnp.zeros((2 * width, 2 * width), summed.dtype), term.astype(summed.dtype), (offset, offset))
    nothing = jnp.zeros((width, width), summed.dtype)
    upper = jnp.stack([nothing, dense[:width, :width], dense[:width, width:]])
    lower = jnp.stack([dense[width:, :width], dense[width:, width:], nothing])
    increment = jnp.stack([upper, lower])
    paired = lax.dynamic_slice_in_dim(summed, lead, 2, 0)
    return lax.dynamic_update_slice_in_dim(summed, paired + increment, lead, 0)

def reference(density, pattern, windows, basis_values, basis_grads, weights):
    kept = (pattern > 0)[:, :, None, None]
    current = jnp.where(kept, density, jnp.zeros_like(density))
    for iteration in range(ITERS):
        padded = jnp.pad(current, ((2, 2), (0, 0), (0, 0), (0, 0)))
        square = jnp.where(kept, band_product(current, padded), 0.0).astype(jnp.bfloat16)
        cubic = band_product(square, padded)
        current = jnp.where(kept, 3.0 * square.astype(jnp.float32) - 2.0 * cubic, 0.0).astype(jnp.bfloat16)
    near = current[:, 1:4]

    def one_tile(tile_index, carry):
        summed, densities = carry
        position = tile_index.astype(jnp.int32)
        start_step = windows[position]
        lead = (start_step // 2).astype(jnp.int32)
        offset = (start_step % 2 * HB).astype(jnp.int32)
        window_block = window_of(near, lead, offset, FN)
        values = lax.dynamic_index_in_dim(basis_values, position, 0, keepdims=False)
        grads = lax.dynamic_index_in_dim(basis_grads, position, 1, keepdims=False)
        quadrature = lax.dynamic_index_in_dim(weights, position, 0, keepdims=False)
        point_density, contribution = tile_terms(values, grads, quadrature, window_block)
        summed = spread_term(summed, contribution, lead, offset)
        densities = lax.dynamic_update_index_in_dim(densities, point_density, position, 0)
        return (summed, densities)
    start_carry = (jnp.zeros((BLOCKS, 3, BS, BS), jnp.float32), jnp.zeros((NTILES, POINTS), jnp.float32))
    summed, densities = lax.fori_loop(0, NTILES, one_tile, start_carry)
    xc_matrix = jnp.where(kept, jnp.pad(summed, ((0, 0), (1, 1), (0, 0), (0, 0))), 0.0)
    return (current, xc_matrix, densities)
```

```python
import jax
import jax.numpy as jnp
from jax import lax
from jax.experimental import pallas as pl
from jax.experimental.pallas import tpu as pltpu
from jax.sharding import PartitionSpec as P

ITERS = 2


slater_cx = 0.7386
kappa_pbe = 0.804
mu_pbe = 0.2195


def padded(cells, sides, width):
    for axis, dim in sides:
        count = lax.axis_size(axis)
        ends = count - 1
        head = lax.slice_in_dim(cells, 0, width, axis=dim)
        tail = lax.slice_in_dim(cells, cells.shape[dim] - width, cells.shape[dim], axis=dim)
        cells = jnp.concatenate(
            [
                lax.ppermute(tail, axis, [(i, (i + 1) % count) for i in range(ends)]),
                cells,
                lax.ppermute(head, axis, [((i + 1) % count, i) for i in range(ends)]),
            ],
            axis=dim,
        )
    return cells


def shifted_2(value, axis, by):
    length = lax.axis_size(axis)
    pairs = [(i, i + by) for i in range(length) if 0 <= i + by < length]
    return lax.ppermute(value, axis, pairs)


def pointwise(n,g,w,points):
    u=n*n+1.0
    lu=jnp.log(u)
    a=jnp.exp(lu*(2.0/3.0))
    ia=1.0/a
    b=ia*ia
    sig=g[0]*g[0]+g[1]*g[1]+g[2]*g[2]
    t=sig*b
    iden=1.0/(1.0+(mu_pbe/kappa_pbe)*t)
    fac=1.0+kappa_pbe-kappa_pbe*iden
    dF=mu_pbe*iden*iden
    vs=-slater_cx*dF*ia
    vn=-slater_cx*a*(n/u)*((4.0/3.0)*fac-(8.0/3.0)*t*dF)
    sc=w*(1.0/points)
    c0=0.5*vn*sc
    s2=2.0*vs*sc
    return c0,[s2*gk for gk in g]
def tile_kernel(points, v_ref, g_ref, w_ref, win_ref, dens_ref, term_ref, vs_ref, z_ref, y_ref):
    i=pl.program_id(0); n=pl.num_programs(0)-1
    tp,fn=v_ref.shape
    nb=tp//128
    def stage_a():
        win=win_ref[...]
        lane=lax.broadcasted_iota(jnp.int32,(128,128),1)
        m=jnp.zeros((128,128),jnp.float32)
        for b in range(nb):
            v=v_ref[128*b:128*b+128]
            x=jnp.dot(v,win,preferred_element_type=jnp.float32)
            m=jnp.where(lane==b,jnp.sum(x*v.astype(jnp.float32),axis=1,keepdims=True),m)
            for k in range(3):
                gk=g_ref[k,128*b:128*b+128].astype(jnp.float32)
                m=jnp.where(lane==nb*(k+1)+b,jnp.sum(x*gk,axis=1,keepdims=True),m)
        mt=m.T
        nd=mt[0:nb]*(1.0/fn)
        g=[mt[nb*(k+1):nb*(k+2)]*(2.0/fn) for k in range(3)]
        dens_ref[...]=nd
        c0,ck=pointwise(nd,g,w_ref[...],points)
        c=jnp.concatenate([c0]+ck+[jnp.zeros((128-4*nb,128),jnp.float32)],axis=0).T
        for b in range(nb):
            v=v_ref[128*b:128*b+128]
            z=c[:,b:b+1]*v.astype(jnp.float32)
            for k in range(3):
                z=z+c[:,nb*(k+1)+b:nb*(k+1)+b+1]*g_ref[k,128*b:128*b+128].astype(jnp.float32)
            z_ref[i%2,128*b:128*b+128]=z.astype(jnp.bfloat16)
            vs_ref[i%2,128*b:128*b+128]=v
    def stage_b(first):
        y=lax.dot_general(vs_ref[(i+1)%2],z_ref[(i+1)%2],(((0,),(0,)),((),())),preferred_element_type=jnp.float32)
        y_ref[...]=y if first else y_ref[...]+y
    @pl.when(i==0)
    def _(): stage_a()
    @pl.when(i==1)
    def _():
        stage_b(True); stage_a()
    @pl.when((i>1)&(i<n))
    def _():
        stage_b(False); stage_a()
    @pl.when(i==n)
    def _():
        stage_b(False)
        y=y_ref[...]
        term_ref[...]=y+y.T
def tile_call(t, basis_values, basis_grads, wts, window, tp=1024):
    points,fn=basis_values.shape[1:]
    nch=points//tp; nb=tp//128
    cl=lambda i: jnp.minimum(i,nch-1)
    return pl.pallas_call(lambda *r: tile_kernel(points,*r),
      grid=(nch+1,),
      in_specs=[pl.BlockSpec((None,tp,fn),lambda i:(t,cl(i),0)),
                pl.BlockSpec((3,None,tp,fn),lambda i:(0,t,cl(i),0)),
                pl.BlockSpec((None,nb,128),lambda i:(t,cl(i),0)),
                pl.BlockSpec((fn,fn),lambda i:(0,0))],
      out_specs=[pl.BlockSpec((nb,128),lambda i:(cl(i),0)),pl.BlockSpec((fn,fn),lambda i:(0,0))],
      out_shape=[jax.ShapeDtypeStruct((points//128,128),jnp.float32),jax.ShapeDtypeStruct((fn,fn),jnp.float32)],
      scratch_shapes=[pltpu.VMEM((2,tp,fn),jnp.bfloat16),pltpu.VMEM((2,tp,fn),jnp.bfloat16),pltpu.VMEM((fn,fn),jnp.float32)],
      compiler_params=pltpu.CompilerParams(vmem_limit_bytes=48<<20),
      name="tile")(basis_values,basis_grads,wts,window)

def band_product(left, right_padded):
    blocks = left.shape[0]
    total = None
    for offset_step in range(5):
        shifted = right_padded[offset_step : offset_step + blocks]
        widened = jnp.pad(shifted, ((0, 0), (2, 2), (0, 0), (0, 0)))
        picked = widened[:, 4 - offset_step : 9 - offset_step]
        term = jnp.einsum(
            "brk,bdkc->bdrc", left[:, offset_step], picked, preferred_element_type=jnp.float32
        )
        total = term if total is None else total + term
    return total


def window_of(band_three, lead, offset, functions):
    paired = lax.dynamic_slice_in_dim(band_three, lead, 2, 0)
    upper = jnp.concatenate([paired[0, 1], paired[0, 2]], axis=1)
    lower = jnp.concatenate([paired[1, 0], paired[1, 1]], axis=1)
    dense = jnp.concatenate([upper, lower], axis=0)
    return lax.dynamic_slice(dense, (offset, offset), (functions, functions))


def spread_term(summed, term, lead, offset):
    width = summed.shape[2]
    dense = lax.dynamic_update_slice(
        jnp.zeros((2 * width, 2 * width), summed.dtype), term, (offset, offset)
    )
    nothing = jnp.zeros((width, width), summed.dtype)
    upper = jnp.stack([nothing, dense[:width, :width], dense[:width, width:]])
    lower = jnp.stack([dense[width:, :width], dense[width:, width:], nothing])
    increment = jnp.stack([upper, lower])
    paired = lax.dynamic_slice_in_dim(summed, lead, 2, 0)
    return lax.dynamic_update_slice_in_dim(summed, paired + increment, lead, 0)


def times_current(left, current):
    near_right = padded(current, (("row", 0),), 2)
    return band_product(left, lax.all_gather(near_right, "col", axis=2, tiled=True))


def edge_rows(summed):
    blocks = summed.shape[0] - 2
    from_above = shifted_2(summed[0].astype(jnp.bfloat16), "row", -1).astype(jnp.float32)
    from_below = shifted_2(summed[blocks + 1].astype(jnp.bfloat16), "row", 1).astype(jnp.float32)
    own_rows = summed[1 : blocks + 1]
    return jnp.concatenate(
        [
            own_rows[:1] + from_below[None],
            own_rows[1 : blocks - 1],
            own_rows[blocks - 1 :] + from_above[None],
        ],
        axis=0,
    )


def on_device(density, pattern, windows, basis_values, basis_grads, weights):
    row_index = lax.axis_index("row")
    band_rows = density.shape[0]
    functions = basis_values.shape[2]
    step_size = functions // 3
    kept = (pattern > 0)[:, :, None, None]
    current = jnp.where(kept, density, jnp.zeros_like(density))
    for iteration in range(ITERS):
        square = jnp.where(kept, times_current(current, current), 0.0).astype(jnp.bfloat16)
        cubic = times_current(square, current)
        current = jnp.where(kept, 3.0 * square.astype(jnp.float32) - 2.0 * cubic, 0.0).astype(
            jnp.bfloat16
        )
    rows_full = lax.all_gather(current, "col", axis=2, tiled=True)
    near_full = padded(rows_full, (("row", 0),), 1)
    near = near_full[:, 1:4]
    tiles_here = windows.shape[0]
    points = basis_values.shape[1]
    block_size = near.shape[2]

    summed = jnp.zeros((band_rows + 2, 3, block_size, block_size), jnp.float32)
    quadrature = weights.reshape(tiles_here, points // 128, 128)
    densities = []
    for tile in range(tiles_here):
        start_step = windows[tile]
        lead = start_step // 2 - (band_rows * row_index - 1)
        offset = start_step % 2 * step_size
        window_block = window_of(near, lead, offset, functions)
        density_rows, contribution = tile_call(tile, basis_values, basis_grads, quadrature, window_block)
        summed = spread_term(summed, contribution, lead, offset)
        densities.append(density_rows.reshape(points))
    densities = jnp.stack(densities)
    local_terms = summed
    owner_part = lax.psum_scatter(
        local_terms.astype(jnp.bfloat16), "col", scatter_dimension=2, tiled=True
    ).astype(jnp.float32)
    mine = edge_rows(owner_part)
    xc_matrix = jnp.where(kept, jnp.pad(mine, ((0, 0), (1, 1), (0, 0), (0, 0))), 0.0)
    return (current, xc_matrix, densities)


def solution(mesh):
    placed = (
        P("row", None, "col", None),
        P("row", None),
        P(("row", "col")),
        P(("row", "col"), None, None),
        P(None, ("row", "col"), None, None),
        P(("row", "col"), None),
    )
    return jax.shard_map(
        on_device,
        mesh=mesh,
        in_specs=placed,
        out_specs=(
            P("row", None, "col", None),
            P("row", None, "col", None),
            P(("row", "col"), None),
        ),
        check_vma=False,
    )
```

```python
import jax
import jax.numpy as jnp
from jax import lax
from jax.experimental import pallas as pl
from jax.experimental.pallas import tpu as pltpu
from jax.sharding import PartitionSpec as P

ITERS = 2


slater_cx = 0.7386
kappa_pbe = 0.804
mu_pbe = 0.2195


def padded(cells, sides, width):
    for axis, dim in sides:
        count = lax.axis_size(axis)
        ends = count - 1
        head = lax.slice_in_dim(cells, 0, width, axis=dim)
        tail = lax.slice_in_dim(cells, cells.shape[dim] - width, cells.shape[dim], axis=dim)
        cells = jnp.concatenate(
            [
                lax.ppermute(tail, axis, [(i, (i + 1) % count) for i in range(ends)]),
                cells,
                lax.ppermute(head, axis, [((i + 1) % count, i) for i in range(ends)]),
            ],
            axis=dim,
        )
    return cells


def shifted_2(value, axis, by):
    length = lax.axis_size(axis)
    pairs = [(i, i + by) for i in range(length) if 0 <= i + by < length]
    return lax.ppermute(value, axis, pairs)


def energy_sum(point_density, grad_square):
    spread = jnp.sqrt(point_density * point_density + 1.0)
    reduced = grad_square / spread ** (8.0 / 3.0)
    enhance = 1.0 + kappa_pbe - kappa_pbe / (1.0 + mu_pbe * reduced / kappa_pbe)
    return jnp.sum(-slater_cx * spread ** (4.0 / 3.0) * enhance)


def tile_terms(values, grads, quadrature, window_block):
    functions = values.shape[1]
    points = values.shape[0]
    projected = jnp.dot(values, window_block, preferred_element_type=jnp.float32)
    point_density = jnp.sum(projected * values.astype(jnp.float32), axis=1) / functions
    slopes = 2.0 * jnp.sum(projected[None] * grads.astype(jnp.float32), axis=2) / functions
    grad_square = jnp.sum(slopes * slopes, axis=0)
    by_density, by_gradient = jax.grad(energy_sum, argnums=(0, 1))(point_density, grad_square)
    scaled = quadrature / points
    weighted = (0.5 * by_density * scaled)[:, None] * values.astype(jnp.float32)
    weighted = weighted + jnp.sum(
        ((2.0 * by_gradient * scaled)[None] * slopes)[:, :, None] * grads.astype(jnp.float32),
        axis=0,
    )
    weighted = weighted.astype(jnp.bfloat16)
    one_side = lax.dot_general(
        values, weighted, (((0,), (0,)), ((), ())), preferred_element_type=jnp.float32
    )
    return (point_density, one_side + one_side.T)


def band_product(left, right_padded):
    blocks = left.shape[0]
    total = None
    for offset_step in range(5):
        shifted = right_padded[offset_step : offset_step + blocks]
        widened = jnp.pad(shifted, ((0, 0), (2, 2), (0, 0), (0, 0)))
        picked = widened[:, 4 - offset_step : 9 - offset_step]
        term = jnp.einsum(
            "brk,bdkc->bdrc", left[:, offset_step], picked, preferred_element_type=jnp.float32
        )
        total = term if total is None else total + term
    return total


def window_of(band_three, lead, offset, functions):
    paired = lax.dynamic_slice_in_dim(band_three, lead, 2, 0)
    upper = jnp.concatenate([paired[0, 1], paired[0, 2]], axis=1)
    lower = jnp.concatenate([paired[1, 0], paired[1, 1]], axis=1)
    dense = jnp.concatenate([upper, lower], axis=0)
    return lax.dynamic_slice(dense, (offset, offset), (functions, functions))


def spread_term(summed, term, lead, offset):
    width = summed.shape[2]
    dense = lax.dynamic_update_slice(
        jnp.zeros((2 * width, 2 * width), summed.dtype), term, (offset, offset)
    )
    nothing = jnp.zeros((width, width), summed.dtype)
    upper = jnp.stack([nothing, dense[:width, :width], dense[:width, width:]])
    lower = jnp.stack([dense[width:, :width], dense[width:, width:], nothing])
    increment = jnp.stack([upper, lower])
    paired = lax.dynamic_slice_in_dim(summed, lead, 2, 0)
    return lax.dynamic_update_slice_in_dim(summed, paired + increment, lead, 0)


def times_current(left, current):
    near_right = padded(current, (("row", 0),), 2)
    return band_product(left, lax.all_gather(near_right, "col", axis=2, tiled=True))


def edge_rows(summed):
    blocks = summed.shape[0] - 2
    from_above = shifted_2(summed[0].astype(jnp.bfloat16), "row", -1).astype(jnp.float32)
    from_below = shifted_2(summed[blocks + 1].astype(jnp.bfloat16), "row", 1).astype(jnp.float32)
    own_rows = summed[1 : blocks + 1]
    return jnp.concatenate(
        [
            own_rows[:1] + from_below[None],
            own_rows[1 : blocks - 1],
            own_rows[blocks - 1 :] + from_above[None],
        ],
        axis=0,
    )


def by_gathers(density, pattern, windows, basis_values, basis_grads, weights):
    row_index = lax.axis_index("row")
    band_rows = density.shape[0]
    functions = basis_values.shape[2]
    step_size = functions // 3
    kept = (pattern > 0)[:, :, None, None]
    current = jnp.where(kept, density, jnp.zeros_like(density))
    for iteration in range(ITERS):
        square = jnp.where(kept, times_current(current, current), 0.0).astype(jnp.bfloat16)
        cubic = times_current(square, current)
        current = jnp.where(kept, 3.0 * square.astype(jnp.float32) - 2.0 * cubic, 0.0).astype(
            jnp.bfloat16
        )
    rows_full = lax.all_gather(current, "col", axis=2, tiled=True)
    near_full = padded(rows_full, (("row", 0),), 1)
    near = near_full[:, 1:4]
    tiles_here = windows.shape[0]
    points = basis_values.shape[1]
    block_size = near.shape[2]

    def one_tile(tile_index, carry):
        summed, densities = carry
        position = tile_index.astype(jnp.int32)
        start_step = windows[position]
        lead = start_step // 2 - (band_rows * row_index - 1)
        offset = start_step % 2 * step_size
        window_block = window_of(near, lead, offset, functions)
        values = lax.dynamic_index_in_dim(basis_values, position, 0, keepdims=False)
        grads = lax.dynamic_index_in_dim(basis_grads, position, 1, keepdims=False)
        quadrature = lax.dynamic_index_in_dim(weights, position, 0, keepdims=False)
        point_density, contribution = tile_terms(values, grads, quadrature, window_block)
        summed = spread_term(summed, contribution, lead, offset)
        densities = lax.dynamic_update_index_in_dim(densities, point_density, position, 0)
        return (summed, densities)

    start_carry = (
        jnp.zeros((band_rows + 2, 3, block_size, block_size), jnp.float32),
        jnp.zeros((tiles_here, points), jnp.float32),
    )
    local_terms, densities = lax.fori_loop(0, tiles_here, one_tile, start_carry)
    owner_part = lax.psum_scatter(
        local_terms.astype(jnp.bfloat16), "col", scatter_dimension=2, tiled=True
    ).astype(jnp.float32)
    mine = edge_rows(owner_part)
    xc_matrix = jnp.where(kept, jnp.pad(mine, ((0, 0), (1, 1), (0, 0), (0, 0))), 0.0)
    return (current, xc_matrix, densities)


BF16 = jnp.bfloat16
F32 = jnp.float32


def mixed(index, turn, count):
    return index ^ turn if count & (count - 1) == 0 else (turn - index) % count


class Chain:
    def __init__(self, rows, cols):
        self.rows, self.cols, self.count = rows, cols, rows * cols

    def device(self, block_row):
        pair, step = divmod(block_row, 2 * self.cols)
        plane, core = divmod(step, 2)
        plane = plane if pair % 2 == 0 else self.cols - 1 - plane
        return (2 * pair + core) * self.cols + plane

    def step(self, row_index, col_index):
        pair, core = row_index // 2, row_index % 2
        plane = jnp.where(pair % 2 == 0, col_index, self.cols - 1 - col_index)
        return 2 * plane + core

    def to_rows(self, turn):
        pairs = []
        for row in range(self.rows):
            for col in range(self.cols):
                pairs.append((row * self.cols + col, self.device(row * self.cols + mixed(col, turn, self.cols))))
        return pairs

    def to_slices(self, turn):
        return [(b, a) for a, b in self.to_rows(turn)]

    def shift(self, by):
        return [(self.device(i), self.device(i + by)) for i in range(self.count) if 0 <= i + by < self.count]


BOTH = ("row", "col")
VMEM_SPEC = pl.BlockSpec(memory_space=pltpu.VMEM)
SMEM_SPEC = pl.BlockSpec(memory_space=pltpu.SMEM)


def small_call(body, name, scalars, arrays, outs, scratch=()):
    return pl.pallas_call(
        body,
        in_specs=[SMEM_SPEC] * len(scalars) + [VMEM_SPEC] * len(arrays),
        out_specs=[VMEM_SPEC] * len(outs),
        out_shape=[jax.ShapeDtypeStruct(s, d) for s, d in outs],
        scratch_shapes=[pltpu.VMEM(s, d) for s, d in scratch],
        compiler_params=pltpu.CompilerParams(vmem_limit_bytes=48 << 20),
        name=name,
    )(*scalars, *arrays)


SENDS = ((1, 5), (2, 5), (0, 4), (0, 3))


def join_rows(pieces, place, block):
    cols = len(pieces)
    high = block // cols

    def body(place_ref, *refs):
        ins, outs = refs[:cols], refs[cols:]
        for turn in range(cols):
            at = pl.ds(pl.multiple_of(mixed(place_ref[0], turn, cols) * high, high), high)
            for d in range(5):
                value = ins[turn][d]
                outs[0][d, at] = value
                for out, (low, top) in zip(outs[1:], SENDS):
                    if low <= d < top:
                        out[d - low, at] = value

    shapes = [((5, block, block), BF16)] + [((top - low, block, block), BF16) for low, top in SENDS]
    return small_call(body, "join_rows", [place], pieces, shapes)


def exchange_rows(chain, sends):
    return [lax.ppermute(s, BOTH, chain.shift(by)) for s, by in zip(sends, (1, 2, -1, -2))]


def purify(own, near, kept, place, block, cols, last):
    high = block // cols

    def body(kept_ref, place_ref, own_ref, m1, m2, p1, p2, *refs):
        outs, square = refs[:-1], refs[-1]

        def right(o, far):
            return (m2, m1, own_ref, p1, p2)[o + 2][far + (2, 2, 2, 1, 0)[o + 2]]

        def product(left, d):
            far, total = d - 2, None
            for o in range(max(-2, far - 2), min(2, far + 2) + 1):
                term = jnp.dot(left[o + 2], right(o, far), preferred_element_type=F32)
                total = term if total is None else total + term
            return jnp.where(kept_ref[d] > 0, total, 0.0)

        for d in range(5):
            square[d] = product(own_ref, d).astype(BF16)
        for d in range(5):
            value = 3.0 * square[d].astype(F32) - 2.0 * product(square, d)
            value = value.astype(BF16)
            if last:
                outs[-1][d] = value
            else:
                outs[0][d] = value
                for out, (low, top) in zip(outs[1:], SENDS):
                    if low <= d < top:
                        out[d - low] = value
        if last:
            for turn in range(cols):
                at = pl.ds(pl.multiple_of(mixed(place_ref[0], turn, cols) * high, high), high)
                for d in range(5):
                    outs[turn][d] = outs[-1][d, at]

    whole = ((5, block, block), BF16)
    if last:
        shapes = [((5, high, block), BF16)] * cols + [whole]
    else:
        shapes = [whole] + [((top - low, block, block), BF16) for low, top in SENDS]
    outs = small_call(body, "purify", [kept, place], [own] + list(near), shapes, [whole])
    return outs[:cols] if last else outs


def join_slices(pieces, place, block):
    cols = len(pieces)
    high = block // cols

    def body(place_ref, *refs):
        ins, (out, down, up) = refs[:cols], refs[cols:]
        for turn in range(cols):
            out[mixed(place_ref[0], turn, cols)] = ins[turn][...]
        down[...] = out[cols - 1, 2:4]
        up[...] = out[0, 1:3]

    edge = ((2, high, block), BF16)
    return small_call(body, "join_slices", [place], pieces, [((cols, 5, high, block), BF16), edge, edge])


def slot_of(step, half):
    offset = step % 2
    first = (half - offset + 2) % 2
    return offset, first, (offset + first) // 2


def pack_windows(purified, above, below, steps, place, tiles, functions):
    cols, _, high, block = purified.shape
    part = functions // 3
    per_half = part // high

    def body(steps_ref, place_ref, pur, above_ref, below_ref, *refs):
        outs, near = refs[:-1], refs[-1]
        for low in range(2):
            for b in range(2):
                at = slice(b * block, (b + 1) * block)
                for row in range(cols + 2):
                    if low == 0 and row == 0:
                        near[low, row, :, at] = above_ref[b]
                    elif low == 1 and row == cols + 1:
                        near[low, row, :, at] = below_ref[b]
                    elif 0 < row < cols + 1:
                        near[low, row, :, at] = pur[row - 1, 2 - low + b]
        half = place_ref[0] // per_half
        for to in range(cols):
            for tile in range(tiles):
                step = steps_ref[to, tile]
                offset, _, low = slot_of(step, half)
                lanes = pl.ds(pl.multiple_of(offset * part, part), functions)
                outs[tile][to, 0] = near[low, step // 2 + low, :, lanes]
                outs[tile][to, 1] = near[1, step // 2 + 1, :, lanes]

    return small_call(
        body, "pack_windows", [steps, place], [purified, above, below],
        [((cols, 2, high, functions), BF16)] * tiles, [((2, cols + 2, high, 2 * block), BF16)],
    )


def pointwise(n, g, w, points):
    u = n * n + 1.0
    a = jnp.exp(jnp.log(u) * (2.0 / 3.0))
    ia = 1.0 / a
    t = (g[0] * g[0] + g[1] * g[1] + g[2] * g[2]) * (ia * ia)
    part = 1.0 / (1.0 + (mu_pbe / kappa_pbe) * t)
    enhance = 1.0 + kappa_pbe - kappa_pbe * part
    slope = mu_pbe * part * part
    by_gradient = -slater_cx * slope * ia
    by_density = -slater_cx * a * (n / u) * ((4.0 / 3.0) * enhance - (8.0 / 3.0) * t * slope)
    scaled = w * (1.0 / points)
    return 0.5 * by_density * scaled, [2.0 * by_gradient * scaled * gk for gk in g]


def tile_call(tile, basis_values, basis_grads, quadrature, pieces, step, rows=1024):
    points, functions = basis_values.shape[1:]
    cols, _, high, _ = pieces.shape
    part = functions // 3
    per_half = part // high
    count, blocks = points // rows, rows // 128

    def body(step_ref, v_ref, g_ref, w_ref, pieces_ref, dens_ref, term_ref, win_ref, vs_ref, z_ref, y_ref):
        i = pl.program_id(0)
        offset = step_ref[0] % 2

        @pl.when(i == 0)
        def _():
            for h in range(3):
                for sub in range(per_half):
                    source = per_half * ((offset + h) % 2) + sub
                    win_ref[part * h + high * sub : part * h + high * (sub + 1)] = pieces_ref[source, h // 2]

        def forward():
            window = win_ref[...]
            lane = lax.broadcasted_iota(jnp.int32, (128, 128), 1)
            sums = jnp.zeros((128, 128), F32)
            for b in range(blocks):
                at = slice(128 * b, 128 * (b + 1))
                v = v_ref[at]
                x = jnp.dot(v, window, preferred_element_type=F32)
                sums = jnp.where(lane == b, jnp.sum(x * v.astype(F32), axis=1, keepdims=True), sums)
                for k in range(3):
                    gk = g_ref[k, at].astype(F32)
                    sums = jnp.where(lane == blocks * (k + 1) + b, jnp.sum(x * gk, axis=1, keepdims=True), sums)
            sums = sums.T
            n = sums[:blocks] * (1.0 / functions)
            g = [sums[blocks * (k + 1) : blocks * (k + 2)] * (2.0 / functions) for k in range(3)]
            dens_ref[...] = n
            c0, ck = pointwise(n, g, w_ref[...], points)
            c = jnp.concatenate([c0] + ck + [jnp.zeros((128 - 4 * blocks, 128), F32)], axis=0).T
            for b in range(blocks):
                at = slice(128 * b, 128 * (b + 1))
                v = v_ref[at]
                z = c[:, b : b + 1] * v.astype(F32)
                for k in range(3):
                    col = blocks * (k + 1) + b
                    z = z + c[:, col : col + 1] * g_ref[k, at].astype(F32)
                z_ref[i % 2, at] = z.astype(BF16)
                vs_ref[i % 2, at] = v

        def backward(first):
            y = lax.dot_general(
                vs_ref[(i + 1) % 2], z_ref[(i + 1) % 2], (((0,), (0,)), ((), ())), preferred_element_type=F32
            )
            y_ref[...] = y if first else y_ref[...] + y

        @pl.when(i == 0)
        def _():
            forward()

        @pl.when(i == 1)
        def _():
            backward(True)
            forward()

        @pl.when((i > 1) & (i < count))
        def _():
            backward(False)
            forward()

        @pl.when(i == count)
        def _():
            backward(False)
            y = y_ref[...]
            y_ref[...] = y + y.T
            for to in range(cols):
                _, first, _ = slot_of(step_ref[0], to // per_half)
                start = pl.multiple_of(part * first + high * (to % per_half), high)
                term_ref[to, 0] = y_ref[pl.ds(start, high)].astype(BF16)
                start = 2 * part + high * (to % per_half)
                term_ref[to, 1] = y_ref[start : start + high].astype(BF16)

    def chunk(i):
        return jnp.minimum(i, count - 1)

    return pl.pallas_call(
        body,
        grid=(count + 1,),
        in_specs=[
            SMEM_SPEC,
            pl.BlockSpec((None, rows, functions), lambda i: (tile, chunk(i), 0)),
            pl.BlockSpec((3, None, rows, functions), lambda i: (0, tile, chunk(i), 0)),
            pl.BlockSpec((None, blocks, 128), lambda i: (tile, chunk(i), 0)),
            pl.BlockSpec(pieces.shape, lambda i: (0, 0, 0, 0)),
        ],
        out_specs=[
            pl.BlockSpec((blocks, 128), lambda i: (chunk(i), 0)),
            pl.BlockSpec(pieces.shape, lambda i: (0, 0, 0, 0)),
        ],
        out_shape=[
            jax.ShapeDtypeStruct((points // 128, 128), F32),
            jax.ShapeDtypeStruct(pieces.shape, BF16),
        ],
        scratch_shapes=[
            pltpu.VMEM((functions, functions), BF16),
            pltpu.VMEM((2, rows, functions), BF16),
            pltpu.VMEM((2, rows, functions), BF16),
            pltpu.VMEM((functions, functions), F32),
        ],
        compiler_params=pltpu.CompilerParams(vmem_limit_bytes=48 << 20),
        name="tile",
    )(step, basis_values, basis_grads, quadrature, pieces)


def add_terms(terms, steps, place, block):
    tiles = len(terms)
    cols, _, high, functions = terms[0].shape
    part = functions // 3
    per_half = part // high

    def body(steps_ref, place_ref, *refs):
        ins, (own, to_above, to_below, total) = refs[:tiles], refs[tiles:]
        total[...] = jnp.zeros(total.shape, F32)
        half = place_ref[0] // per_half
        for source in range(cols):
            for tile in range(tiles):
                step = steps_ref[source, tile]
                offset, first, low = slot_of(step, half)
                lanes = pl.ds(pl.multiple_of(offset * part, part), functions)
                total[low, step // 2 + low, :, lanes] += ins[tile][source, 0].astype(F32)

                @pl.when(first == 0)
                def _():
                    total[1, step // 2 + 1, :, lanes] += ins[tile][source, 1].astype(F32)

        for row in range(1, cols + 1):
            own[row - 1, 0] = total[1, row, :, :block]
            own[row - 1, 1] = total[1, row, :, block:] + total[0, row, :, :block]
            own[row - 1, 2] = total[0, row, :, block:]
        for b in range(2):
            at = slice(b * block, (b + 1) * block)
            to_above[b] = total[0, 0, :, at].astype(BF16)
            to_below[b] = total[1, cols + 1, :, at].astype(BF16)

    edge = ((2, high, block), BF16)
    return small_call(
        body, "add_terms", [steps, place], list(terms),
        [((cols, 3, high, block), F32), edge, edge], [((2, cols + 2, high, 2 * block), F32)],
    )


def by_block_rows(density, pattern, windows, basis_values, basis_grads, weights):
    rows, cols = lax.axis_size("row"), lax.axis_size("col")
    row_index, col_index = lax.axis_index("row"), lax.axis_index("col")
    block = density.shape[3]
    tiles, points, functions = basis_values.shape
    chain = Chain(rows, cols)
    step_here = chain.step(row_index, col_index)
    place = (step_here % cols).astype(jnp.int32).reshape(1)
    slice_here = col_index.astype(jnp.int32).reshape(1)
    kept = (pattern > 0)[:, :, None, None]
    masked = jnp.where(kept, density, jnp.zeros_like(density))
    pieces = []
    for turn in range(cols):
        piece = lax.dynamic_index_in_dim(masked, mixed(col_index, turn, cols), 0, keepdims=False)
        pieces.append(lax.ppermute(piece, BOTH, chain.to_rows(turn)))
    other = lax.ppermute(pattern, "row", [(i, i ^ 1) for i in range(rows)])
    pattern_two = jnp.where(
        row_index % 2 == 0, jnp.concatenate([pattern, other]), jnp.concatenate([other, pattern])
    )
    kept_row = lax.dynamic_index_in_dim(pattern_two, step_here, 0, keepdims=False)
    steps_here = (windows - (2 * cols * row_index - 2)).astype(jnp.int32)
    steps = lax.all_to_all(jnp.broadcast_to(steps_here, (cols, tiles)), "col", 0, 0, tiled=True)

    own, *sends = join_rows(pieces, place, block)
    for iteration in range(ITERS):
        near = exchange_rows(chain, sends)
        out = purify(own, near, kept_row, place, block, cols, iteration == ITERS - 1)
        own, sends = out[0], out[1:]
    pieces = [lax.ppermute(p, BOTH, chain.to_slices(turn)) for turn, p in enumerate(out)]
    purified, down, up = join_slices(pieces, slice_here, block)
    above = shifted_2(down, "row", 1)
    below = shifted_2(up, "row", -1)
    sent = pack_windows(purified, above, below, steps, slice_here, tiles, functions)

    quadrature = weights.reshape(tiles, points // 128, 128)
    densities, terms = [], []
    for tile in range(tiles):
        window = lax.all_to_all(sent[tile], "col", 0, 0, tiled=True)
        dens, term = tile_call(
            tile, basis_values, basis_grads, quadrature, window, steps_here[tile : tile + 1]
        )
        densities.append(dens.reshape(points))
        terms.append(lax.all_to_all(term, "col", 0, 0, tiled=True))
    mine, to_above, to_below = add_terms(terms, steps, slice_here, block)
    from_below = shifted_2(to_above, "row", -1).astype(F32)
    from_above = shifted_2(to_below, "row", 1).astype(F32)
    first = jnp.pad(from_above[None], ((0, cols - 1), (0, 1), (0, 0), (0, 0)))
    last = jnp.pad(from_below[None], ((cols - 1, 0), (1, 0), (0, 0), (0, 0)))
    summed = mine + first + last
    xc_matrix = jnp.where(kept, jnp.pad(summed, ((0, 0), (1, 1), (0, 0), (0, 0))), 0.0)
    return purified, xc_matrix, jnp.stack(densities)


def on_device(density, pattern, windows, basis_values, basis_grads, weights):
    rows, cols = lax.axis_size("row"), lax.axis_size("col")
    band_rows, block, functions = density.shape[0], density.shape[3], basis_values.shape[2]
    fits = (
        band_rows == cols
        and rows % 2 == 0
        and 2 * functions == 3 * block
        and functions // 3 % density.shape[2] == 0
        and basis_values.shape[1] % 1024 == 0
    )
    plan = by_block_rows if fits else by_gathers
    return plan(density, pattern, windows, basis_values, basis_grads, weights)


def solution(mesh):
    placed = (
        P("row", None, "col", None),
        P("row", None),
        P(("row", "col")),
        P(("row", "col"), None, None),
        P(None, ("row", "col"), None, None),
        P(("row", "col"), None),
    )
    return jax.shard_map(
        on_device,
        mesh=mesh,
        in_specs=placed,
        out_specs=(
            P("row", None, "col", None),
            P("row", None, "col", None),
            P(("row", "col"), None),
        ),
        check_vma=False,
    )
```

```python
import jax
import jax.numpy as jnp
from jax import lax
from jax.experimental import pallas as pl
from jax.experimental.pallas import tpu as pltpu
from jax.sharding import PartitionSpec as P

ITERS = 2


slater_cx = 0.7386
kappa_pbe = 0.804
mu_pbe = 0.2195


def padded(cells, sides, width):
    for axis, dim in sides:
        count = lax.axis_size(axis)
        ends = count - 1
        head = lax.slice_in_dim(cells, 0, width, axis=dim)
        tail = lax.slice_in_dim(cells, cells.shape[dim] - width, cells.shape[dim], axis=dim)
        cells = jnp.concatenate(
            [
                lax.ppermute(tail, axis, [(i, (i + 1) % count) for i in range(ends)]),
                cells,
                lax.ppermute(head, axis, [((i + 1) % count, i) for i in range(ends)]),
            ],
            axis=dim,
        )
    return cells


def shifted_2(value, axis, by):
    length = lax.axis_size(axis)
    pairs = [(i, i + by) for i in range(length) if 0 <= i + by < length]
    return lax.ppermute(value, axis, pairs)


def energy_sum(point_density, grad_square):
    spread = jnp.sqrt(point_density * point_density + 1.0)
    reduced = grad_square / spread ** (8.0 / 3.0)
    enhance = 1.0 + kappa_pbe - kappa_pbe / (1.0 + mu_pbe * reduced / kappa_pbe)
    return jnp.sum(-slater_cx * spread ** (4.0 / 3.0) * enhance)


def tile_terms(values, grads, quadrature, window_block):
    functions = values.shape[1]
    points = values.shape[0]
    projected = jnp.dot(values, window_block, preferred_element_type=jnp.float32)
    point_density = jnp.sum(projected * values.astype(jnp.float32), axis=1) / functions
    slopes = 2.0 * jnp.sum(projected[None] * grads.astype(jnp.float32), axis=2) / functions
    grad_square = jnp.sum(slopes * slopes, axis=0)
    by_density, by_gradient = jax.grad(energy_sum, argnums=(0, 1))(point_density, grad_square)
    scaled = quadrature / points
    weighted = (0.5 * by_density * scaled)[:, None] * values.astype(jnp.float32)
    weighted = weighted + jnp.sum(
        ((2.0 * by_gradient * scaled)[None] * slopes)[:, :, None] * grads.astype(jnp.float32),
        axis=0,
    )
    weighted = weighted.astype(jnp.bfloat16)
    one_side = lax.dot_general(
        values, weighted, (((0,), (0,)), ((), ())), preferred_element_type=jnp.float32
    )
    return (point_density, one_side + one_side.T)


def band_product(left, right_padded):
    blocks = left.shape[0]
    total = None
    for offset_step in range(5):
        shifted = right_padded[offset_step : offset_step + blocks]
        widened = jnp.pad(shifted, ((0, 0), (2, 2), (0, 0), (0, 0)))
        picked = widened[:, 4 - offset_step : 9 - offset_step]
        term = jnp.einsum(
            "brk,bdkc->bdrc", left[:, offset_step], picked, preferred_element_type=jnp.float32
        )
        total = term if total is None else total + term
    return total


def window_of(band_three, lead, offset, functions):
    paired = lax.dynamic_slice_in_dim(band_three, lead, 2, 0)
    upper = jnp.concatenate([paired[0, 1], paired[0, 2]], axis=1)
    lower = jnp.concatenate([paired[1, 0], paired[1, 1]], axis=1)
    dense = jnp.concatenate([upper, lower], axis=0)
    return lax.dynamic_slice(dense, (offset, offset), (functions, functions))


def spread_term(summed, term, lead, offset):
    width = summed.shape[2]
    dense = lax.dynamic_update_slice(
        jnp.zeros((2 * width, 2 * width), summed.dtype), term, (offset, offset)
    )
    nothing = jnp.zeros((width, width), summed.dtype)
    upper = jnp.stack([nothing, dense[:width, :width], dense[:width, width:]])
    lower = jnp.stack([dense[width:, :width], dense[width:, width:], nothing])
    increment = jnp.stack([upper, lower])
    paired = lax.dynamic_slice_in_dim(summed, lead, 2, 0)
    return lax.dynamic_update_slice_in_dim(summed, paired + increment, lead, 0)


def times_current(left, current):
    near_right = padded(current, (("row", 0),), 2)
    return band_product(left, lax.all_gather(near_right, "col", axis=2, tiled=True))


def edge_rows(summed):
    blocks = summed.shape[0] - 2
    from_above = shifted_2(summed[0].astype(jnp.bfloat16), "row", -1).astype(jnp.float32)
    from_below = shifted_2(summed[blocks + 1].astype(jnp.bfloat16), "row", 1).astype(jnp.float32)
    own_rows = summed[1 : blocks + 1]
    return jnp.concatenate(
        [
            own_rows[:1] + from_below[None],
            own_rows[1 : blocks - 1],
            own_rows[blocks - 1 :] + from_above[None],
        ],
        axis=0,
    )


def by_gathers(density, pattern, windows, basis_values, basis_grads, weights):
    row_index = lax.axis_index("row")
    band_rows = density.shape[0]
    functions = basis_values.shape[2]
    step_size = functions // 3
    kept = (pattern > 0)[:, :, None, None]
    current = jnp.where(kept, density, jnp.zeros_like(density))
    for iteration in range(ITERS):
        square = jnp.where(kept, times_current(current, current), 0.0).astype(jnp.bfloat16)
        cubic = times_current(square, current)
        current = jnp.where(kept, 3.0 * square.astype(jnp.float32) - 2.0 * cubic, 0.0).astype(
            jnp.bfloat16
        )
    rows_full = lax.all_gather(current, "col", axis=2, tiled=True)
    near_full = padded(rows_full, (("row", 0),), 1)
    near = near_full[:, 1:4]
    tiles_here = windows.shape[0]
    points = basis_values.shape[1]
    block_size = near.shape[2]

    def one_tile(tile_index, carry):
        summed, densities = carry
        position = tile_index.astype(jnp.int32)
        start_step = windows[position]
        lead = start_step // 2 - (band_rows * row_index - 1)
        offset = start_step % 2 * step_size
        window_block = window_of(near, lead, offset, functions)
        values = lax.dynamic_index_in_dim(basis_values, position, 0, keepdims=False)
        grads = lax.dynamic_index_in_dim(basis_grads, position, 1, keepdims=False)
        quadrature = lax.dynamic_index_in_dim(weights, position, 0, keepdims=False)
        point_density, contribution = tile_terms(values, grads, quadrature, window_block)
        summed = spread_term(summed, contribution, lead, offset)
        densities = lax.dynamic_update_index_in_dim(densities, point_density, position, 0)
        return (summed, densities)

    start_carry = (
        jnp.zeros((band_rows + 2, 3, block_size, block_size), jnp.float32),
        jnp.zeros((tiles_here, points), jnp.float32),
    )
    local_terms, densities = lax.fori_loop(0, tiles_here, one_tile, start_carry)
    owner_part = lax.psum_scatter(
        local_terms.astype(jnp.bfloat16), "col", scatter_dimension=2, tiled=True
    ).astype(jnp.float32)
    mine = edge_rows(owner_part)
    xc_matrix = jnp.where(kept, jnp.pad(mine, ((0, 0), (1, 1), (0, 0), (0, 0))), 0.0)
    return (current, xc_matrix, densities)


BF16 = jnp.bfloat16
F32 = jnp.float32


def mixed(index, turn, count):
    return index ^ turn if count & (count - 1) == 0 else (turn - index) % count


class Chain:
    def __init__(self, rows, cols):
        self.rows, self.cols, self.count = rows, cols, rows * cols

    def device(self, block_row):
        pair, step = divmod(block_row, 2 * self.cols)
        plane, core = divmod(step, 2)
        plane = plane if pair % 2 == 0 else self.cols - 1 - plane
        return (2 * pair + core) * self.cols + plane

    def step(self, row_index, col_index):
        pair, core = row_index // 2, row_index % 2
        plane = jnp.where(pair % 2 == 0, col_index, self.cols - 1 - col_index)
        return 2 * plane + core

    def to_rows(self, turn):
        pairs = []
        for row in range(self.rows):
            for col in range(self.cols):
                pairs.append((row * self.cols + col, self.device(row * self.cols + mixed(col, turn, self.cols))))
        return pairs

    def to_slices(self, turn):
        return [(b, a) for a, b in self.to_rows(turn)]

    def shift(self, by):
        return [(self.device(i), self.device(i + by)) for i in range(self.count) if 0 <= i + by < self.count]


BOTH = ("row", "col")
VMEM_SPEC = pl.BlockSpec(memory_space=pltpu.VMEM)
SMEM_SPEC = pl.BlockSpec(memory_space=pltpu.SMEM)


def small_call(body, name, scalars, arrays, outs, scratch=()):
    return pl.pallas_call(
        body,
        in_specs=[SMEM_SPEC] * len(scalars) + [VMEM_SPEC] * len(arrays),
        out_specs=[VMEM_SPEC] * len(outs),
        out_shape=[jax.ShapeDtypeStruct(s, d) for s, d in outs],
        scratch_shapes=[pltpu.VMEM(s, d) for s, d in scratch],
        compiler_params=pltpu.CompilerParams(vmem_limit_bytes=48 << 20),
        name=name,
    )(*scalars, *arrays)


HELD = (0, 2, 3)
SENDS = ((1, 5), (2, 5), (0, 4), (0, 3))


def join_rows(pieces, steps, place, slice_here, block):
    cols, tiles = len(pieces), steps[0].shape[0]
    high = block // cols

    def body(place_ref, slice_ref, *refs):
        step_ins, ins = refs[:cols], refs[cols : 2 * cols]
        own, up, down, steps_out = refs[2 * cols :]
        for turn in range(cols):
            for tile in range(tiles):
                steps_out[mixed(slice_ref[0], turn, cols), tile] = step_ins[turn][tile]
            at = pl.ds(pl.multiple_of(mixed(place_ref[0], turn, cols) * high, high), high)
            for k in range(3):
                value = ins[turn][k]
                own[k, at] = value
                if k > 0:
                    up[k - 1, at] = value
                if k < 2:
                    down[k, at] = value

    two, three = ((2, block, block), BF16), ((3, block, block), BF16)
    return pl.pallas_call(
        body,
        in_specs=[SMEM_SPEC] * (2 + cols) + [VMEM_SPEC] * cols,
        out_specs=[VMEM_SPEC] * 3 + [SMEM_SPEC],
        out_shape=[jax.ShapeDtypeStruct(*x) for x in (three, two, two, ((cols, tiles), jnp.int32))],
        name="join_rows",
    )(place, slice_here, *steps, *pieces)


def exchange_rows(chain, sends):
    far = [lax.ppermute(s, BOTH, chain.shift(by)) for s, by in zip(sends[1::2], (2, -2))]
    near = [lax.ppermute(s, BOTH, chain.shift(by)) for s, by in zip(sends[0::2], (1, -1))]
    return near[0], far[0], near[1], far[1]


def purify_math(kept_ref, left, right, square, store):
    def product(left, d):
        far, total = d - 2, None
        for o in range(max(-2, far - 2), min(2, far + 2) + 1):
            term = jnp.dot(left(o), right(o, far), preferred_element_type=F32)
            total = term if total is None else total + term
        return jnp.where(kept_ref[d] > 0, total, 0.0)

    for d in range(5):
        square[d] = product(left, d).astype(BF16)
    for d in range(5):
        value = 3.0 * square[d].astype(F32) - 2.0 * product(lambda o: square[o + 2], d)
        store(d, value.astype(BF16))


def purify_first(own, near, kept, block):
    places = [(a, b) for a in range(-2, 3) for b in range(-2, 3) if abs(a - b) <= 2]
    held = [(-2, -2), (-2, -1), (-1, -1), (-1, 0), (0, -2), (0, 0), (0, 1), (1, -1), (1, 1), (1, 2), (2, 0), (2, 2)]
    flipped = [(a, b) for a, b in places if (a, b) not in held]

    def body(kept_ref, own_ref, m1, m2, p1, p2, *refs):
        outs, (square, turned) = refs[:-2], refs[-2:]
        source = [(m2, 0), (m2, 1), (m1, 0), (m1, 1), (own_ref, 0), (own_ref, 1), (own_ref, 2)]
        source += [(p1, 0), (p1, 1), (p1, 2), (p2, 0), (p2, 1)]
        source = dict(zip(held, source))
        for k, (a, b) in enumerate(flipped):
            ref, at = source[b, a]
            turned[k] = ref[at].T
            source[a, b] = (turned, k)

        def block_at(a, b):
            ref, at = source[a, b]
            return ref[at]

        def store(d, value):
            outs[0][d] = value
            for out, (low, top) in zip(outs[1:], SENDS):
                if low <= d < top:
                    out[d - low] = value

        purify_math(kept_ref, lambda o: block_at(0, o), block_at, square, store)

    whole = ((5, block, block), BF16)
    shapes = [whole] + [((top - low, block, block), BF16) for low, top in SENDS]
    scratch = [whole, ((len(flipped), block, block), BF16)]
    return small_call(body, "purify_first", [kept], [own] + list(near), shapes, scratch)


def purify_next(own, near, kept, block, place, cols):
    high = block // cols
    last = place is not None

    def body(kept_ref, *refs):
        place_ref, refs = (refs[0], refs[1:]) if last else (None, refs)
        own_ref, m1, m2, p1, p2 = refs[:5]
        outs, square = refs[5:-1], refs[-1]

        def right(o, far):
            return (m2, m1, own_ref, p1, p2)[o + 2][far + (2, 2, 2, 1, 0)[o + 2]]

        def store(d, value):
            if last:
                outs[-1][d] = value
                return
            outs[0][d] = value
            for out, (low, top) in zip(outs[1:], SENDS):
                if low <= d < top:
                    out[d - low] = value

        purify_math(kept_ref, lambda o: own_ref[o + 2], right, square, store)
        if last:
            for turn in range(cols):
                at = pl.ds(pl.multiple_of(mixed(place_ref[0], turn, cols) * high, high), high)
                for d in range(5):
                    outs[turn][d] = outs[-1][d, at]

    whole = ((5, block, block), BF16)
    if last:
        shapes = [((5, high, block), BF16)] * cols + [whole]
    else:
        shapes = [whole] + [((top - low, block, block), BF16) for low, top in SENDS]
    outs = small_call(body, "purify", [kept] + ([place] if last else []), [own] + list(near), shapes, [whole])
    return outs[:cols] if last else outs


def join_slices(pieces, place, block):
    cols = len(pieces)
    high = block // cols

    def body(place_ref, *refs):
        ins, (out, down, up) = refs[:cols], refs[cols:]
        for turn in range(cols):
            out[mixed(place_ref[0], turn, cols)] = ins[turn][...]
        down[...] = out[cols - 1, 2:4]
        up[...] = out[0, 1:3]

    edge = ((2, high, block), BF16)
    return small_call(body, "join_slices", [place], pieces, [((cols, 5, high, block), BF16), edge, edge])


def slot_of(step, half):
    offset = step % 2
    first = (half - offset + 2) % 2
    return offset, first, (offset + first) // 2


def pack_windows(purified, above, below, steps, place, tiles, functions):
    cols, _, high, block = purified.shape
    part = functions // 3
    per_half = part // high

    def body(steps_ref, place_ref, pur, above_ref, below_ref, *refs):
        outs, near = refs[:-1], refs[-1]
        for low in range(2):
            for b in range(2):
                at = slice(b * block, (b + 1) * block)
                for row in range(cols + 2):
                    if low == 0 and row == 0:
                        near[low, row, :, at] = above_ref[b]
                    elif low == 1 and row == cols + 1:
                        near[low, row, :, at] = below_ref[b]
                    elif 0 < row < cols + 1:
                        near[low, row, :, at] = pur[row - 1, 2 - low + b]
        half = place_ref[0] // per_half
        for to in range(cols):
            for tile in range(tiles):
                step = steps_ref[to, tile]
                offset, _, low = slot_of(step, half)
                lanes = pl.ds(pl.multiple_of(offset * part, part), functions)
                outs[tile][to, 0] = near[low, step // 2 + low, :, lanes]
                outs[tile][to, 1] = near[1, step // 2 + 1, :, lanes]

    return small_call(
        body, "pack_windows", [steps, place], [purified, above, below],
        [((cols, 2, high, functions), BF16)] * tiles, [((2, cols + 2, high, 2 * block), BF16)],
    )


def pointwise(n, g, w, points):
    u = n * n + 1.0
    a = jnp.exp(jnp.log(u) * (2.0 / 3.0))
    ia = 1.0 / a
    t = (g[0] * g[0] + g[1] * g[1] + g[2] * g[2]) * (ia * ia)
    part = 1.0 / (1.0 + (mu_pbe / kappa_pbe) * t)
    enhance = 1.0 + kappa_pbe - kappa_pbe * part
    slope = mu_pbe * part * part
    by_gradient = -slater_cx * slope * ia
    by_density = -slater_cx * a * (n / u) * ((4.0 / 3.0) * enhance - (8.0 / 3.0) * t * slope)
    scaled = w * (1.0 / points)
    return 0.5 * by_density * scaled, [2.0 * by_gradient * scaled * gk for gk in g]


def tile_call(tile, basis_values, basis_grads, quadrature, pieces, step, rows=1024):
    points, functions = basis_values.shape[1:]
    cols, _, high, _ = pieces.shape
    part = functions // 3
    per_half = part // high
    count, blocks = points // rows, rows // 128

    def body(step_ref, v_ref, g_ref, w_ref, pieces_ref, dens_ref, term_ref, win_ref, vs_ref, z_ref, y_ref):
        i = pl.program_id(0)
        offset = step_ref[0] % 2

        @pl.when(i == 0)
        def _():
            for h in range(3):
                for sub in range(per_half):
                    source = per_half * ((offset + h) % 2) + sub
                    win_ref[part * h + high * sub : part * h + high * (sub + 1)] = pieces_ref[source, h // 2]

        def forward():
            window = win_ref[...]
            lane = lax.broadcasted_iota(jnp.int32, (128, 128), 1)
            sums = jnp.zeros((128, 128), F32)
            for b in range(blocks):
                at = slice(128 * b, 128 * (b + 1))
                v = v_ref[at]
                x = jnp.dot(v, window, preferred_element_type=F32)
                sums = jnp.where(lane == b, jnp.sum(x * v.astype(F32), axis=1, keepdims=True), sums)
                for k in range(3):
                    gk = g_ref[k, at].astype(F32)
                    sums = jnp.where(lane == blocks * (k + 1) + b, jnp.sum(x * gk, axis=1, keepdims=True), sums)
            sums = sums.T
            n = sums[:blocks] * (1.0 / functions)
            g = [sums[blocks * (k + 1) : blocks * (k + 2)] * (2.0 / functions) for k in range(3)]
            dens_ref[...] = n
            c0, ck = pointwise(n, g, w_ref[...], points)
            c = jnp.concatenate([c0] + ck + [jnp.zeros((128 - 4 * blocks, 128), F32)], axis=0).T
            for b in range(blocks):
                at = slice(128 * b, 128 * (b + 1))
                v = v_ref[at]
                z = c[:, b : b + 1] * v.astype(F32)
                for k in range(3):
                    col = blocks * (k + 1) + b
                    z = z + c[:, col : col + 1] * g_ref[k, at].astype(F32)
                z_ref[i % 2, at] = z.astype(BF16)
                vs_ref[i % 2, at] = v

        def backward(first):
            y = lax.dot_general(
                vs_ref[(i + 1) % 2], z_ref[(i + 1) % 2], (((0,), (0,)), ((), ())), preferred_element_type=F32
            )
            y_ref[...] = y if first else y_ref[...] + y

        @pl.when(i == 0)
        def _():
            forward()

        @pl.when(i == 1)
        def _():
            backward(True)
            forward()

        @pl.when((i > 1) & (i < count))
        def _():
            backward(False)
            forward()

        @pl.when(i == count)
        def _():
            backward(False)
            y = y_ref[...]
            y_ref[...] = y + y.T
            for to in range(cols):
                _, first, _ = slot_of(step_ref[0], to // per_half)
                start = pl.multiple_of(part * first + high * (to % per_half), high)
                term_ref[to, 0] = y_ref[pl.ds(start, high)].astype(BF16)
                start = 2 * part + high * (to % per_half)
                term_ref[to, 1] = y_ref[start : start + high].astype(BF16)

    def chunk(i):
        return jnp.minimum(i, count - 1)

    return pl.pallas_call(
        body,
        grid=(count + 1,),
        in_specs=[
            SMEM_SPEC,
            pl.BlockSpec((None, rows, functions), lambda i: (tile, chunk(i), 0)),
            pl.BlockSpec((3, None, rows, functions), lambda i: (0, tile, chunk(i), 0)),
            pl.BlockSpec((None, blocks, 128), lambda i: (tile, chunk(i), 0)),
            pl.BlockSpec(pieces.shape, lambda i: (0, 0, 0, 0)),
        ],
        out_specs=[
            pl.BlockSpec((blocks, 128), lambda i: (chunk(i), 0)),
            pl.BlockSpec(pieces.shape, lambda i: (0, 0, 0, 0)),
        ],
        out_shape=[
            jax.ShapeDtypeStruct((points // 128, 128), F32),
            jax.ShapeDtypeStruct(pieces.shape, BF16),
        ],
        scratch_shapes=[
            pltpu.VMEM((functions, functions), BF16),
            pltpu.VMEM((2, rows, functions), BF16),
            pltpu.VMEM((2, rows, functions), BF16),
            pltpu.VMEM((functions, functions), F32),
        ],
        compiler_params=pltpu.CompilerParams(vmem_limit_bytes=48 << 20),
        name="tile",
    )(step, basis_values, basis_grads, quadrature, pieces)


def add_terms(terms, steps, place, block):
    tiles = len(terms)
    cols, _, high, functions = terms[0].shape
    part = functions // 3
    per_half = part // high

    def body(steps_ref, place_ref, *refs):
        ins, (own, to_above, to_below, total) = refs[:tiles], refs[tiles:]
        total[...] = jnp.zeros(total.shape, F32)
        half = place_ref[0] // per_half
        for source in range(cols):
            for tile in range(tiles):
                step = steps_ref[source, tile]
                offset, first, low = slot_of(step, half)
                lanes = pl.ds(pl.multiple_of(offset * part, part), functions)
                total[low, step // 2 + low, :, lanes] += ins[tile][source, 0].astype(F32)

                @pl.when(first == 0)
                def _():
                    total[1, step // 2 + 1, :, lanes] += ins[tile][source, 1].astype(F32)

        for row in range(1, cols + 1):
            own[row - 1, 0] = total[1, row, :, :block]
            own[row - 1, 1] = total[1, row, :, block:] + total[0, row, :, :block]
            own[row - 1, 2] = total[0, row, :, block:]
        for b in range(2):
            at = slice(b * block, (b + 1) * block)
            to_above[b] = total[0, 0, :, at].astype(BF16)
            to_below[b] = total[1, cols + 1, :, at].astype(BF16)

    edge = ((2, high, block), BF16)
    return small_call(
        body, "add_terms", [steps, place], list(terms),
        [((cols, 3, high, block), F32), edge, edge], [((2, cols + 2, high, 2 * block), F32)],
    )


def by_block_rows(density, pattern, windows, basis_values, basis_grads, weights):
    rows, cols = lax.axis_size("row"), lax.axis_size("col")
    row_index, col_index = lax.axis_index("row"), lax.axis_index("col")
    block = density.shape[3]
    tiles, points, functions = basis_values.shape
    chain = Chain(rows, cols)
    step_here = chain.step(row_index, col_index)
    place = (step_here % cols).astype(jnp.int32).reshape(1)
    slice_here = col_index.astype(jnp.int32).reshape(1)
    kept = (pattern > 0)[:, :, None, None]
    masked = jnp.where(kept, density, jnp.zeros_like(density))
    held = jnp.stack([masked[:, d] for d in HELD], axis=1)
    pieces = []
    for turn in range(cols):
        piece = lax.dynamic_index_in_dim(held, mixed(col_index, turn, cols), 0, keepdims=False)
        pieces.append(lax.ppermute(piece, BOTH, chain.to_rows(turn)))
    other = lax.ppermute(pattern, "row", [(i, i ^ 1) for i in range(rows)])
    pattern_two = jnp.where(
        row_index % 2 == 0, jnp.concatenate([pattern, other]), jnp.concatenate([other, pattern])
    )
    kept_row = lax.dynamic_index_in_dim(pattern_two, step_here, 0, keepdims=False)
    steps_here = (windows - (2 * cols * row_index - 2)).astype(jnp.int32)
    rounds = [[(i, mixed(i, turn, cols)) for i in range(cols)] for turn in range(cols)]
    steps = [
        steps_here if all(a == b for a, b in pairs) else lax.ppermute(steps_here, "col", pairs) for pairs in rounds
    ]
    own, up, down, steps = join_rows(pieces, steps, place, slice_here, block)
    sends = (up, up, own, down)
    for iteration in range(ITERS):
        near = exchange_rows(chain, sends)
        last = place if iteration == ITERS - 1 else None
        if iteration == 0:
            out = purify_first(own, near, kept_row, block)
        else:
            out = purify_next(own, near, kept_row, block, last, cols)
        own, sends = out[0], out[1:]
    pieces = [lax.ppermute(p, BOTH, chain.to_slices(turn)) for turn, p in enumerate(out)]
    purified, down, up = join_slices(pieces, slice_here, block)
    above = shifted_2(down, "row", 1)
    below = shifted_2(up, "row", -1)
    sent = pack_windows(purified, above, below, steps, slice_here, tiles, functions)

    quadrature = weights.reshape(tiles, points // 128, 128)
    densities, terms = [], []
    for tile in range(tiles):
        window = lax.all_to_all(sent[tile], "col", 0, 0, tiled=True)
        dens, term = tile_call(
            tile, basis_values, basis_grads, quadrature, window, steps_here[tile : tile + 1]
        )
        densities.append(dens.reshape(points))
        terms.append(lax.all_to_all(term, "col", 0, 0, tiled=True))
    mine, to_above, to_below = add_terms(terms, steps, slice_here, block)
    from_below = shifted_2(to_above, "row", -1).astype(F32)
    from_above = shifted_2(to_below, "row", 1).astype(F32)
    first = jnp.pad(from_above[None], ((0, cols - 1), (0, 1), (0, 0), (0, 0)))
    last = jnp.pad(from_below[None], ((cols - 1, 0), (1, 0), (0, 0), (0, 0)))
    summed = mine + first + last
    xc_matrix = jnp.where(kept, jnp.pad(summed, ((0, 0), (1, 1), (0, 0), (0, 0))), 0.0)
    return purified, xc_matrix, jnp.stack(densities)


def on_device(density, pattern, windows, basis_values, basis_grads, weights):
    rows, cols = lax.axis_size("row"), lax.axis_size("col")
    band_rows, block, functions = density.shape[0], density.shape[3], basis_values.shape[2]
    fits = (
        band_rows == cols
        and rows % 2 == 0
        and 2 * functions == 3 * block
        and functions // 3 % density.shape[2] == 0
        and basis_values.shape[1] % 1024 == 0
    )
    plan = by_block_rows if fits else by_gathers
    return plan(density, pattern, windows, basis_values, basis_grads, weights)


def solution(mesh):
    placed = (
        P("row", None, "col", None),
        P("row", None),
        P(("row", "col")),
        P(("row", "col"), None, None),
        P(None, ("row", "col"), None, None),
        P(("row", "col"), None),
    )
    return jax.shard_map(
        on_device,
        mesh=mesh,
        in_specs=placed,
        out_specs=(
            P("row", None, "col", None),
            P("row", None, "col", None),
            P(("row", "col"), None),
        ),
        check_vma=False,
    )
```

```python
import jax
import jax.numpy as jnp
from jax import lax
from jax.experimental import pallas as pl
from jax.experimental.pallas import tpu as pltpu
from jax.sharding import PartitionSpec as P

ITERS = 2


slater_cx = 0.7386
kappa_pbe = 0.804
mu_pbe = 0.2195


def padded(cells, sides, width):
    for axis, dim in sides:
        count = lax.axis_size(axis)
        ends = count - 1
        head = lax.slice_in_dim(cells, 0, width, axis=dim)
        tail = lax.slice_in_dim(cells, cells.shape[dim] - width, cells.shape[dim], axis=dim)
        cells = jnp.concatenate(
            [
                lax.ppermute(tail, axis, [(i, (i + 1) % count) for i in range(ends)]),
                cells,
                lax.ppermute(head, axis, [((i + 1) % count, i) for i in range(ends)]),
            ],
            axis=dim,
        )
    return cells


def shifted_2(value, axis, by):
    length = lax.axis_size(axis)
    pairs = [(i, i + by) for i in range(length) if 0 <= i + by < length]
    return lax.ppermute(value, axis, pairs)


def energy_sum(point_density, grad_square):
    spread = jnp.sqrt(point_density * point_density + 1.0)
    reduced = grad_square / spread ** (8.0 / 3.0)
    enhance = 1.0 + kappa_pbe - kappa_pbe / (1.0 + mu_pbe * reduced / kappa_pbe)
    return jnp.sum(-slater_cx * spread ** (4.0 / 3.0) * enhance)


def tile_terms(values, grads, quadrature, window_block):
    functions = values.shape[1]
    points = values.shape[0]
    projected = jnp.dot(values, window_block, preferred_element_type=jnp.float32)
    point_density = jnp.sum(projected * values.astype(jnp.float32), axis=1) / functions
    slopes = 2.0 * jnp.sum(projected[None] * grads.astype(jnp.float32), axis=2) / functions
    grad_square = jnp.sum(slopes * slopes, axis=0)
    by_density, by_gradient = jax.grad(energy_sum, argnums=(0, 1))(point_density, grad_square)
    scaled = quadrature / points
    weighted = (0.5 * by_density * scaled)[:, None] * values.astype(jnp.float32)
    weighted = weighted + jnp.sum(
        ((2.0 * by_gradient * scaled)[None] * slopes)[:, :, None] * grads.astype(jnp.float32),
        axis=0,
    )
    weighted = weighted.astype(jnp.bfloat16)
    one_side = lax.dot_general(
        values, weighted, (((0,), (0,)), ((), ())), preferred_element_type=jnp.float32
    )
    return (point_density, one_side + one_side.T)


def band_product(left, right_padded):
    blocks = left.shape[0]
    total = None
    for offset_step in range(5):
        shifted = right_padded[offset_step : offset_step + blocks]
        widened = jnp.pad(shifted, ((0, 0), (2, 2), (0, 0), (0, 0)))
        picked = widened[:, 4 - offset_step : 9 - offset_step]
        term = jnp.einsum(
            "brk,bdkc->bdrc", left[:, offset_step], picked, preferred_element_type=jnp.float32
        )
        total = term if total is None else total + term
    return total


def window_of(band_three, lead, offset, functions):
    paired = lax.dynamic_slice_in_dim(band_three, lead, 2, 0)
    upper = jnp.concatenate([paired[0, 1], paired[0, 2]], axis=1)
    lower = jnp.concatenate([paired[1, 0], paired[1, 1]], axis=1)
    dense = jnp.concatenate([upper, lower], axis=0)
    return lax.dynamic_slice(dense, (offset, offset), (functions, functions))


def spread_term(summed, term, lead, offset):
    width = summed.shape[2]
    dense = lax.dynamic_update_slice(
        jnp.zeros((2 * width, 2 * width), summed.dtype), term, (offset, offset)
    )
    nothing = jnp.zeros((width, width), summed.dtype)
    upper = jnp.stack([nothing, dense[:width, :width], dense[:width, width:]])
    lower = jnp.stack([dense[width:, :width], dense[width:, width:], nothing])
    increment = jnp.stack([upper, lower])
    paired = lax.dynamic_slice_in_dim(summed, lead, 2, 0)
    return lax.dynamic_update_slice_in_dim(summed, paired + increment, lead, 0)


def times_current(left, current):
    near_right = padded(current, (("row", 0),), 2)
    return band_product(left, lax.all_gather(near_right, "col", axis=2, tiled=True))


def edge_rows(summed):
    blocks = summed.shape[0] - 2
    from_above = shifted_2(summed[0].astype(jnp.bfloat16), "row", -1).astype(jnp.float32)
    from_below = shifted_2(summed[blocks + 1].astype(jnp.bfloat16), "row", 1).astype(jnp.float32)
    own_rows = summed[1 : blocks + 1]
    return jnp.concatenate(
        [
            own_rows[:1] + from_below[None],
            own_rows[1 : blocks - 1],
            own_rows[blocks - 1 :] + from_above[None],
        ],
        axis=0,
    )


def by_gathers(density, pattern, windows, basis_values, basis_grads, weights):
    row_index = lax.axis_index("row")
    band_rows = density.shape[0]
    functions = basis_values.shape[2]
    step_size = functions // 3
    kept = (pattern > 0)[:, :, None, None]
    current = jnp.where(kept, density, jnp.zeros_like(density))
    for iteration in range(ITERS):
        square = jnp.where(kept, times_current(current, current), 0.0).astype(jnp.bfloat16)
        cubic = times_current(square, current)
        current = jnp.where(kept, 3.0 * square.astype(jnp.float32) - 2.0 * cubic, 0.0).astype(
            jnp.bfloat16
        )
    rows_full = lax.all_gather(current, "col", axis=2, tiled=True)
    near_full = padded(rows_full, (("row", 0),), 1)
    near = near_full[:, 1:4]
    tiles_here = windows.shape[0]
    points = basis_values.shape[1]
    block_size = near.shape[2]

    def one_tile(tile_index, carry):
        summed, densities = carry
        position = tile_index.astype(jnp.int32)
        start_step = windows[position]
        lead = start_step // 2 - (band_rows * row_index - 1)
        offset = start_step % 2 * step_size
        window_block = window_of(near, lead, offset, functions)
        values = lax.dynamic_index_in_dim(basis_values, position, 0, keepdims=False)
        grads = lax.dynamic_index_in_dim(basis_grads, position, 1, keepdims=False)
        quadrature = lax.dynamic_index_in_dim(weights, position, 0, keepdims=False)
        point_density, contribution = tile_terms(values, grads, quadrature, window_block)
        summed = spread_term(summed, contribution, lead, offset)
        densities = lax.dynamic_update_index_in_dim(densities, point_density, position, 0)
        return (summed, densities)

    start_carry = (
        jnp.zeros((band_rows + 2, 3, block_size, block_size), jnp.float32),
        jnp.zeros((tiles_here, points), jnp.float32),
    )
    local_terms, densities = lax.fori_loop(0, tiles_here, one_tile, start_carry)
    owner_part = lax.psum_scatter(
        local_terms.astype(jnp.bfloat16), "col", scatter_dimension=2, tiled=True
    ).astype(jnp.float32)
    mine = edge_rows(owner_part)
    xc_matrix = jnp.where(kept, jnp.pad(mine, ((0, 0), (1, 1), (0, 0), (0, 0))), 0.0)
    return (current, xc_matrix, densities)


BF16 = jnp.bfloat16
F32 = jnp.float32


def mixed(index, turn, count):
    return index ^ turn if count & (count - 1) == 0 else (turn - index) % count


class Chain:
    def __init__(self, rows, cols):
        self.rows, self.cols, self.count = rows, cols, rows * cols

    def device(self, block_row):
        pair, step = divmod(block_row, 2 * self.cols)
        plane, core = divmod(step, 2)
        plane = plane if pair % 2 == 0 else self.cols - 1 - plane
        return (2 * pair + core) * self.cols + plane

    def step(self, row_index, col_index):
        pair, core = row_index // 2, row_index % 2
        plane = jnp.where(pair % 2 == 0, col_index, self.cols - 1 - col_index)
        return 2 * plane + core

    def to_rows(self, turn):
        pairs = []
        for row in range(self.rows):
            for col in range(self.cols):
                pairs.append((row * self.cols + col, self.device(row * self.cols + mixed(col, turn, self.cols))))
        return pairs

    def to_slices(self, turn):
        return [(b, a) for a, b in self.to_rows(turn)]

    def shift(self, by):
        return [(self.device(i), self.device(i + by)) for i in range(self.count) if 0 <= i + by < self.count]


BOTH = ("row", "col")
VMEM_SPEC = pl.BlockSpec(memory_space=pltpu.VMEM)
SMEM_SPEC = pl.BlockSpec(memory_space=pltpu.SMEM)


def small_call(body, name, scalars, arrays, outs, scratch=()):
    return pl.pallas_call(
        body,
        in_specs=[SMEM_SPEC] * len(scalars) + [VMEM_SPEC] * len(arrays),
        out_specs=[VMEM_SPEC] * len(outs),
        out_shape=[jax.ShapeDtypeStruct(s, d) for s, d in outs],
        scratch_shapes=[pltpu.VMEM(s, d) for s, d in scratch],
        compiler_params=pltpu.CompilerParams(vmem_limit_bytes=48 << 20),
        name=name,
    )(*scalars, *arrays)


HELD = (0, 2, 3)
SENDS = ((1, 5), (2, 5), (0, 4), (0, 3))
NOTE = 16


def grid_of(shape, axis):
    return lax.broadcasted_iota(jnp.int32, shape, axis)


def prepare(density, pattern, steps, slice_here):
    cols, _, high, block = density.shape
    tiles = steps.shape[0]

    def body(pattern_ref, steps_ref, slice_ref, density_ref, *outs):
        row, lane = grid_of((NOTE, block), 0), grid_of((NOTE, block), 1)
        for turn in range(cols):
            j = mixed(slice_ref[0], turn, cols)
            for k, d in enumerate(HELD):
                value = density_ref[j, d]
                outs[turn][k * high : (k + 1) * high] = jnp.where(pattern_ref[j, d] > 0, value, jnp.zeros_like(value))
            note = jnp.zeros((NOTE, block), F32)
            for d in range(5):
                note = jnp.where((row == 0) & (lane == d), (pattern_ref[j, d] > 0).astype(F32), note)
            for tile in range(tiles):
                note = jnp.where((row == 1) & (lane == tile), steps_ref[tile].astype(F32), note)
            outs[turn][3 * high :] = note.astype(BF16)

    shapes = [((3 * high + NOTE, block), BF16)] * cols
    return small_call(body, "prepare", [pattern, steps, slice_here], [density], shapes)


def join_rows(pieces, place, block):
    cols = len(pieces)
    high = block // cols

    def body(place_ref, *refs):
        ins, (own, up, down, kept, steps) = refs[:cols], refs[cols:]
        row = grid_of((NOTE, block), 0)
        total = jnp.zeros((NOTE, block), F32)
        for turn in range(cols):
            source = mixed(place_ref[0], turn, cols)
            at = pl.ds(pl.multiple_of(source * high, high), high)
            for k in range(3):
                value = ins[turn][k * high : (k + 1) * high]
                own[k, at] = value
                if k > 0:
                    up[k - 1, at] = value
                if k < 2:
                    down[k, at] = value
            note = ins[turn][3 * high :].astype(F32)
            total = jnp.where(row == source, note[1:2], total)
        kept[...] = note
        steps[...] = total.astype(BF16)

    two, three = ((2, block, block), BF16), ((3, block, block), BF16)
    shapes = [three, two, two, ((NOTE, block), F32), ((NOTE, block), BF16)]
    return small_call(body, "join_rows", [place], pieces, shapes)


def exchange_rows(chain, sends):
    far = [lax.ppermute(s, BOTH, chain.shift(by)) for s, by in zip(sends[1::2], (2, -2))]
    near = [lax.ppermute(s, BOTH, chain.shift(by)) for s, by in zip(sends[0::2], (1, -1))]
    return near[0], far[0], near[1], far[1]


def purify_math(kept_ref, left, right, square, store):
    def product(left, d):
        far, total = d - 2, None
        for o in range(max(-2, far - 2), min(2, far + 2) + 1):
            term = jnp.dot(left(o), right(o, far), preferred_element_type=F32)
            total = term if total is None else total + term
        return jnp.where(kept_ref[0:1, d : d + 1] > 0.0, total, 0.0)

    for d in range(5):
        square[d] = product(left, d).astype(BF16)
    for d in range(5):
        value = 3.0 * square[d].astype(F32) - 2.0 * product(lambda o: square[o + 2], d)
        store(d, value.astype(BF16))


def purify_first(own, near, kept, block):
    places = [(a, b) for a in range(-2, 3) for b in range(-2, 3) if abs(a - b) <= 2]
    held = [(-2, -2), (-2, -1), (-1, -1), (-1, 0), (0, -2), (0, 0), (0, 1), (1, -1), (1, 1), (1, 2), (2, 0), (2, 2)]
    flipped = [(a, b) for a, b in places if (a, b) not in held]

    def body(kept_ref, own_ref, m1, m2, p1, p2, *refs):
        outs, (square, turned) = refs[:-2], refs[-2:]
        source = [(m2, 0), (m2, 1), (m1, 0), (m1, 1), (own_ref, 0), (own_ref, 1), (own_ref, 2)]
        source += [(p1, 0), (p1, 1), (p1, 2), (p2, 0), (p2, 1)]
        source = dict(zip(held, source))
        for k, (a, b) in enumerate(flipped):
            ref, at = source[b, a]
            turned[k] = ref[at].T
            source[a, b] = (turned, k)

        def block_at(a, b):
            ref, at = source[a, b]
            return ref[at]

        def store(d, value):
            outs[0][d] = value
            for out, (low, top) in zip(outs[1:], SENDS):
                if low <= d < top:
                    out[d - low] = value

        purify_math(kept_ref, lambda o: block_at(0, o), block_at, square, store)

    whole = ((5, block, block), BF16)
    shapes = [whole] + [((top - low, block, block), BF16) for low, top in SENDS]
    scratch = [whole, ((len(flipped), block, block), BF16)]
    return small_call(body, "purify_first", [], [kept, own] + list(near), shapes, scratch)


def purify_next(own, near, kept, block, place, steps, cols):
    high = block // cols
    last = place is not None

    def body(*refs):
        place_ref, refs = (refs[0], refs[1:]) if last else (None, refs)
        kept_ref, own_ref, m1, m2, p1, p2, steps_ref = refs[:7]
        outs, (square, whole_ref) = refs[7:-2], refs[-2:]

        def right(o, far):
            return (m2, m1, own_ref, p1, p2)[o + 2][far + (2, 2, 2, 1, 0)[o + 2]]

        def store(d, value):
            if last:
                whole_ref[d] = value
                return
            outs[0][d] = value
            for out, (low, top) in zip(outs[1:], SENDS):
                if low <= d < top:
                    out[d - low] = value

        purify_math(kept_ref, lambda o: own_ref[o + 2], right, square, store)
        if last:
            for turn in range(cols):
                at = pl.ds(pl.multiple_of(mixed(place_ref[0], turn, cols) * high, high), high)
                for d in range(5):
                    outs[turn][d * high : (d + 1) * high] = whole_ref[d, at]
                outs[turn][5 * high :] = steps_ref[...]

    whole = ((5, block, block), BF16)
    if last:
        shapes = [((5 * high + NOTE, block), BF16)] * cols
    else:
        shapes = [whole] + [((top - low, block, block), BF16) for low, top in SENDS]
    return small_call(
        body, "purify", [place] if last else [], [kept, own] + list(near) + [steps], shapes, [whole, whole]
    )


def join_slices(pieces, place, tiles, block):
    cols = len(pieces)
    high = block // cols

    def body(place_ref, *refs):
        ins, (out, down, up, steps) = refs[:cols], refs[cols:]
        for turn in range(cols):
            j = mixed(place_ref[0], turn, cols)
            for d in range(5):
                out[j, d] = ins[turn][d * high : (d + 1) * high]
        down[...] = out[cols - 1, 2:4]
        up[...] = out[0, 1:3]
        note = ins[0][5 * high :].astype(F32)
        row, lane = grid_of((NOTE, block), 0), grid_of((NOTE, block), 1)
        for source in range(cols):
            for tile in range(tiles):
                here = jnp.where((row == source) & (lane == tile), note, 0.0)
                steps[source, tile] = jnp.sum(here).astype(jnp.int32)

    edge = jax.ShapeDtypeStruct((2, high, block), BF16)
    return pl.pallas_call(
        body,
        in_specs=[SMEM_SPEC] + [VMEM_SPEC] * cols,
        out_specs=[VMEM_SPEC] * 3 + [SMEM_SPEC],
        out_shape=[
            jax.ShapeDtypeStruct((cols, 5, high, block), BF16), edge, edge,
            jax.ShapeDtypeStruct((cols, tiles), jnp.int32),
        ],
        name="join_slices",
    )(place, *pieces)


def slot_of(step, half):
    offset = step % 2
    first = (half - offset + 2) % 2
    return offset, first, (offset + first) // 2


def pack_windows(purified, above, below, steps, place, tiles, functions):
    cols, _, high, block = purified.shape
    part = functions // 3
    per_half = part // high

    def body(steps_ref, place_ref, pur, above_ref, below_ref, *refs):
        outs, near = refs[:-1], refs[-1]
        for low in range(2):
            for b in range(2):
                at = slice(b * block, (b + 1) * block)
                for row in range(cols + 2):
                    if low == 0 and row == 0:
                        near[low, row, :, at] = above_ref[b]
                    elif low == 1 and row == cols + 1:
                        near[low, row, :, at] = below_ref[b]
                    elif 0 < row < cols + 1:
                        near[low, row, :, at] = pur[row - 1, 2 - low + b]
        half = place_ref[0] // per_half
        for to in range(cols):
            for tile in range(tiles):
                step = steps_ref[to, tile]
                offset, _, low = slot_of(step, half)
                lanes = pl.ds(pl.multiple_of(offset * part, part), functions)
                outs[tile][to, 0] = near[low, step // 2 + low, :, lanes]
                outs[tile][to, 1] = near[1, step // 2 + 1, :, lanes]

    return small_call(
        body, "pack_windows", [steps, place], [purified, above, below],
        [((cols, 2, high, functions), BF16)] * tiles, [((2, cols + 2, high, 2 * block), BF16)],
    )


def pointwise(n, g, w, points):
    u = n * n + 1.0
    a = jnp.exp(jnp.log(u) * (2.0 / 3.0))
    ia = 1.0 / a
    t = (g[0] * g[0] + g[1] * g[1] + g[2] * g[2]) * (ia * ia)
    part = 1.0 / (1.0 + (mu_pbe / kappa_pbe) * t)
    enhance = 1.0 + kappa_pbe - kappa_pbe * part
    slope = mu_pbe * part * part
    by_gradient = -slater_cx * slope * ia
    by_density = -slater_cx * a * (n / u) * ((4.0 / 3.0) * enhance - (8.0 / 3.0) * t * slope)
    scaled = w * (1.0 / points)
    return 0.5 * by_density * scaled, [2.0 * by_gradient * scaled * gk for gk in g]


def tile_call(tile, basis_values, basis_grads, quadrature, pieces, step, rows=1024):
    points, functions = basis_values.shape[1:]
    cols, _, high, _ = pieces.shape
    part = functions // 3
    per_half = part // high
    count, blocks = points // rows, rows // 128

    def body(step_ref, v_ref, g_ref, w_ref, pieces_ref, dens_ref, term_ref, win_ref, vs_ref, z_ref, y_ref):
        i = pl.program_id(0)
        offset = step_ref[0] % 2

        @pl.when(i == 0)
        def _():
            for h in range(3):
                for sub in range(per_half):
                    source = per_half * ((offset + h) % 2) + sub
                    win_ref[part * h + high * sub : part * h + high * (sub + 1)] = pieces_ref[source, h // 2]

        def forward():
            window = win_ref[...]
            lane = lax.broadcasted_iota(jnp.int32, (128, 128), 1)
            sums = jnp.zeros((128, 128), F32)
            for b in range(blocks):
                at = slice(128 * b, 128 * (b + 1))
                v = v_ref[at]
                x = jnp.dot(v, window, preferred_element_type=F32)
                sums = jnp.where(lane == b, jnp.sum(x * v.astype(F32), axis=1, keepdims=True), sums)
                for k in range(3):
                    gk = g_ref[k, at].astype(F32)
                    sums = jnp.where(lane == blocks * (k + 1) + b, jnp.sum(x * gk, axis=1, keepdims=True), sums)
            sums = sums.T
            n = sums[:blocks] * (1.0 / functions)
            g = [sums[blocks * (k + 1) : blocks * (k + 2)] * (2.0 / functions) for k in range(3)]
            dens_ref[...] = n
            c0, ck = pointwise(n, g, w_ref[...], points)
            c = jnp.concatenate([c0] + ck + [jnp.zeros((128 - 4 * blocks, 128), F32)], axis=0).T
            for b in range(blocks):
                at = slice(128 * b, 128 * (b + 1))
                v = v_ref[at]
                z = c[:, b : b + 1] * v.astype(F32)
                for k in range(3):
                    col = blocks * (k + 1) + b
                    z = z + c[:, col : col + 1] * g_ref[k, at].astype(F32)
                z_ref[i % 2, at] = z.astype(BF16)
                vs_ref[i % 2, at] = v

        def backward(first):
            y = lax.dot_general(
                vs_ref[(i + 1) % 2], z_ref[(i + 1) % 2], (((0,), (0,)), ((), ())), preferred_element_type=F32
            )
            y_ref[...] = y if first else y_ref[...] + y

        @pl.when(i == 0)
        def _():
            forward()

        @pl.when(i == 1)
        def _():
            backward(True)
            forward()

        @pl.when((i > 1) & (i < count))
        def _():
            backward(False)
            forward()

        @pl.when(i == count)
        def _():
            backward(False)
            y = y_ref[...]
            y_ref[...] = y + y.T
            for to in range(cols):
                _, first, _ = slot_of(step_ref[0], to // per_half)
                start = pl.multiple_of(part * first + high * (to % per_half), high)
                term_ref[to, 0] = y_ref[pl.ds(start, high)].astype(BF16)
                start = 2 * part + high * (to % per_half)
                term_ref[to, 1] = y_ref[start : start + high].astype(BF16)

    def chunk(i):
        return jnp.minimum(i, count - 1)

    return pl.pallas_call(
        body,
        grid=(count + 1,),
        in_specs=[
            SMEM_SPEC,
            pl.BlockSpec((None, rows, functions), lambda i: (tile, chunk(i), 0)),
            pl.BlockSpec((3, None, rows, functions), lambda i: (0, tile, chunk(i), 0)),
            pl.BlockSpec((None, blocks, 128), lambda i: (tile, chunk(i), 0)),
            pl.BlockSpec(pieces.shape, lambda i: (0, 0, 0, 0)),
        ],
        out_specs=[
            pl.BlockSpec((blocks, 128), lambda i: (chunk(i), 0)),
            pl.BlockSpec(pieces.shape, lambda i: (0, 0, 0, 0)),
        ],
        out_shape=[
            jax.ShapeDtypeStruct((points // 128, 128), F32),
            jax.ShapeDtypeStruct(pieces.shape, BF16),
        ],
        scratch_shapes=[
            pltpu.VMEM((functions, functions), BF16),
            pltpu.VMEM((2, rows, functions), BF16),
            pltpu.VMEM((2, rows, functions), BF16),
            pltpu.VMEM((functions, functions), F32),
        ],
        compiler_params=pltpu.CompilerParams(vmem_limit_bytes=48 << 20),
        name="tile",
    )(step, basis_values, basis_grads, quadrature, pieces)


def add_terms(terms, steps, place, block):
    tiles = len(terms)
    cols, _, high, functions = terms[0].shape
    part = functions // 3
    per_half = part // high

    def body(steps_ref, place_ref, *refs):
        ins, (own, to_above, to_below, total) = refs[:tiles], refs[tiles:]
        total[...] = jnp.zeros(total.shape, F32)
        half = place_ref[0] // per_half
        for source in range(cols):
            for tile in range(tiles):
                step = steps_ref[source, tile]
                offset, first, low = slot_of(step, half)
                lanes = pl.ds(pl.multiple_of(offset * part, part), functions)
                total[low, step // 2 + low, :, lanes] += ins[tile][source, 0].astype(F32)

                @pl.when(first == 0)
                def _():
                    total[1, step // 2 + 1, :, lanes] += ins[tile][source, 1].astype(F32)

        for row in range(1, cols + 1):
            own[row - 1, 0] = total[1, row, :, :block]
            own[row - 1, 1] = total[1, row, :, block:] + total[0, row, :, :block]
            own[row - 1, 2] = total[0, row, :, block:]
        for b in range(2):
            at = slice(b * block, (b + 1) * block)
            to_above[b] = total[0, 0, :, at].astype(BF16)
            to_below[b] = total[1, cols + 1, :, at].astype(BF16)

    edge = ((2, high, block), BF16)
    return small_call(
        body, "add_terms", [steps, place], list(terms),
        [((cols, 3, high, block), F32), edge, edge], [((2, cols + 2, high, 2 * block), F32)],
    )


def by_block_rows(density, pattern, windows, basis_values, basis_grads, weights):
    rows, cols = lax.axis_size("row"), lax.axis_size("col")
    row_index, col_index = lax.axis_index("row"), lax.axis_index("col")
    block = density.shape[3]
    tiles, points, functions = basis_values.shape
    chain = Chain(rows, cols)
    step_here = chain.step(row_index, col_index)
    place = (step_here % cols).astype(jnp.int32).reshape(1)
    slice_here = col_index.astype(jnp.int32).reshape(1)
    kept = (pattern > 0)[:, :, None, None]
    steps_here = (windows - (2 * cols * row_index - 2)).astype(jnp.int32)
    pieces = prepare(density, pattern, steps_here, slice_here)
    pieces = [lax.ppermute(p, BOTH, chain.to_rows(turn)) for turn, p in enumerate(pieces)]
    own, up, down, kept_row, steps = join_rows(pieces, place, block)
    sends = (up, up, own, down)
    for iteration in range(ITERS):
        near = exchange_rows(chain, sends)
        last = place if iteration == ITERS - 1 else None
        if iteration == 0:
            out = purify_first(own, near, kept_row, block)
        else:
            out = purify_next(own, near, kept_row, block, last, steps, cols)
        own, sends = out[0], out[1:]
    pieces = [lax.ppermute(p, BOTH, chain.to_slices(turn)) for turn, p in enumerate(out)]
    purified, down, up, steps = join_slices(pieces, slice_here, tiles, block)
    above = shifted_2(down, "row", 1)
    below = shifted_2(up, "row", -1)
    sent = pack_windows(purified, above, below, steps, slice_here, tiles, functions)

    quadrature = weights.reshape(tiles, points // 128, 128)
    densities, terms = [], []
    for tile in range(tiles):
        window = lax.all_to_all(sent[tile], "col", 0, 0, tiled=True)
        dens, term = tile_call(
            tile, basis_values, basis_grads, quadrature, window, steps_here[tile : tile + 1]
        )
        densities.append(dens.reshape(points))
        terms.append(lax.all_to_all(term, "col", 0, 0, tiled=True))
    mine, to_above, to_below = add_terms(terms, steps, slice_here, block)
    from_below = shifted_2(to_above, "row", -1).astype(F32)
    from_above = shifted_2(to_below, "row", 1).astype(F32)
    first = jnp.pad(from_above[None], ((0, cols - 1), (0, 1), (0, 0), (0, 0)))
    last = jnp.pad(from_below[None], ((cols - 1, 0), (1, 0), (0, 0), (0, 0)))
    summed = mine + first + last
    xc_matrix = jnp.where(kept, jnp.pad(summed, ((0, 0), (1, 1), (0, 0), (0, 0))), 0.0)
    return purified, xc_matrix, jnp.stack(densities)


def on_device(density, pattern, windows, basis_values, basis_grads, weights):
    rows, cols = lax.axis_size("row"), lax.axis_size("col")
    band_rows, block, functions = density.shape[0], density.shape[3], basis_values.shape[2]
    fits = (
        band_rows == cols
        and rows % 2 == 0
        and 2 * functions == 3 * block
        and functions // 3 % density.shape[2] == 0
        and cols <= NOTE
        and 2 * cols + 2 <= 256
        and basis_values.shape[1] % 1024 == 0
    )
    plan = by_block_rows if fits else by_gathers
    return plan(density, pattern, windows, basis_values, basis_grads, weights)


def solution(mesh):
    placed = (
        P("row", None, "col", None),
        P("row", None),
        P(("row", "col")),
        P(("row", "col"), None, None),
        P(None, ("row", "col"), None, None),
        P(("row", "col"), None),
    )
    return jax.shard_map(
        on_device,
        mesh=mesh,
        in_specs=placed,
        out_specs=(
            P("row", None, "col", None),
            P("row", None, "col", None),
            P(("row", "col"), None),
        ),
        check_vma=False,
    )
```

```python
import jax
import jax.numpy as jnp
from jax import lax
from jax.experimental import pallas as pl
from jax.experimental.pallas import tpu as pltpu
from jax.sharding import PartitionSpec as P

ITERS = 2


slater_cx = 0.7386
kappa_pbe = 0.804
mu_pbe = 0.2195


def padded(cells, sides, width):
    for axis, dim in sides:
        count = lax.axis_size(axis)
        ends = count - 1
        head = lax.slice_in_dim(cells, 0, width, axis=dim)
        tail = lax.slice_in_dim(cells, cells.shape[dim] - width, cells.shape[dim], axis=dim)
        cells = jnp.concatenate(
            [
                lax.ppermute(tail, axis, [(i, (i + 1) % count) for i in range(ends)]),
                cells,
                lax.ppermute(head, axis, [((i + 1) % count, i) for i in range(ends)]),
            ],
            axis=dim,
        )
    return cells


def shifted_2(value, axis, by):
    length = lax.axis_size(axis)
    pairs = [(i, i + by) for i in range(length) if 0 <= i + by < length]
    return lax.ppermute(value, axis, pairs)


def energy_sum(point_density, grad_square):
    spread = jnp.sqrt(point_density * point_density + 1.0)
    reduced = grad_square / spread ** (8.0 / 3.0)
    enhance = 1.0 + kappa_pbe - kappa_pbe / (1.0 + mu_pbe * reduced / kappa_pbe)
    return jnp.sum(-slater_cx * spread ** (4.0 / 3.0) * enhance)


def tile_terms(values, grads, quadrature, window_block):
    functions = values.shape[1]
    points = values.shape[0]
    projected = jnp.dot(values, window_block, preferred_element_type=jnp.float32)
    point_density = jnp.sum(projected * values.astype(jnp.float32), axis=1) / functions
    slopes = 2.0 * jnp.sum(projected[None] * grads.astype(jnp.float32), axis=2) / functions
    grad_square = jnp.sum(slopes * slopes, axis=0)
    by_density, by_gradient = jax.grad(energy_sum, argnums=(0, 1))(point_density, grad_square)
    scaled = quadrature / points
    weighted = (0.5 * by_density * scaled)[:, None] * values.astype(jnp.float32)
    weighted = weighted + jnp.sum(
        ((2.0 * by_gradient * scaled)[None] * slopes)[:, :, None] * grads.astype(jnp.float32),
        axis=0,
    )
    weighted = weighted.astype(jnp.bfloat16)
    one_side = lax.dot_general(
        values, weighted, (((0,), (0,)), ((), ())), preferred_element_type=jnp.float32
    )
    return (point_density, one_side + one_side.T)


def band_product(left, right_padded):
    blocks = left.shape[0]
    total = None
    for offset_step in range(5):
        shifted = right_padded[offset_step : offset_step + blocks]
        widened = jnp.pad(shifted, ((0, 0), (2, 2), (0, 0), (0, 0)))
        picked = widened[:, 4 - offset_step : 9 - offset_step]
        term = jnp.einsum(
            "brk,bdkc->bdrc", left[:, offset_step], picked, preferred_element_type=jnp.float32
        )
        total = term if total is None else total + term
    return total


def window_of(band_three, lead, offset, functions):
    paired = lax.dynamic_slice_in_dim(band_three, lead, 2, 0)
    upper = jnp.concatenate([paired[0, 1], paired[0, 2]], axis=1)
    lower = jnp.concatenate([paired[1, 0], paired[1, 1]], axis=1)
    dense = jnp.concatenate([upper, lower], axis=0)
    return lax.dynamic_slice(dense, (offset, offset), (functions, functions))


def spread_term(summed, term, lead, offset):
    width = summed.shape[2]
    dense = lax.dynamic_update_slice(
        jnp.zeros((2 * width, 2 * width), summed.dtype), term, (offset, offset)
    )
    nothing = jnp.zeros((width, width), summed.dtype)
    upper = jnp.stack([nothing, dense[:width, :width], dense[:width, width:]])
    lower = jnp.stack([dense[width:, :width], dense[width:, width:], nothing])
    increment = jnp.stack([upper, lower])
    paired = lax.dynamic_slice_in_dim(summed, lead, 2, 0)
    return lax.dynamic_update_slice_in_dim(summed, paired + increment, lead, 0)


def times_current(left, current):
    near_right = padded(current, (("row", 0),), 2)
    return band_product(left, lax.all_gather(near_right, "col", axis=2, tiled=True))


def edge_rows(summed):
    blocks = summed.shape[0] - 2
    from_above = shifted_2(summed[0].astype(jnp.bfloat16), "row", -1).astype(jnp.float32)
    from_below = shifted_2(summed[blocks + 1].astype(jnp.bfloat16), "row", 1).astype(jnp.float32)
    own_rows = summed[1 : blocks + 1]
    return jnp.concatenate(
        [
            own_rows[:1] + from_below[None],
            own_rows[1 : blocks - 1],
            own_rows[blocks - 1 :] + from_above[None],
        ],
        axis=0,
    )


def by_gathers(density, pattern, windows, basis_values, basis_grads, weights):
    row_index = lax.axis_index("row")
    band_rows = density.shape[0]
    functions = basis_values.shape[2]
    step_size = functions // 3
    kept = (pattern > 0)[:, :, None, None]
    current = jnp.where(kept, density, jnp.zeros_like(density))
    for _ in range(ITERS):
        square = jnp.where(kept, times_current(current, current), 0.0).astype(jnp.bfloat16)
        cubic = times_current(square, current)
        current = jnp.where(kept, 3.0 * square.astype(jnp.float32) - 2.0 * cubic, 0.0).astype(
            jnp.bfloat16
        )
    rows_full = lax.all_gather(current, "col", axis=2, tiled=True)
    near_full = padded(rows_full, (("row", 0),), 1)
    near = near_full[:, 1:4]
    tiles_here = windows.shape[0]
    points = basis_values.shape[1]
    block_size = near.shape[2]

    def one_tile(tile_index, carry):
        summed, densities = carry
        position = tile_index.astype(jnp.int32)
        start_step = windows[position]
        lead = start_step // 2 - (band_rows * row_index - 1)
        offset = start_step % 2 * step_size
        window_block = window_of(near, lead, offset, functions)
        values = lax.dynamic_index_in_dim(basis_values, position, 0, keepdims=False)
        grads = lax.dynamic_index_in_dim(basis_grads, position, 1, keepdims=False)
        quadrature = lax.dynamic_index_in_dim(weights, position, 0, keepdims=False)
        point_density, contribution = tile_terms(values, grads, quadrature, window_block)
        summed = spread_term(summed, contribution, lead, offset)
        densities = lax.dynamic_update_index_in_dim(densities, point_density, position, 0)
        return (summed, densities)

    start_carry = (
        jnp.zeros((band_rows + 2, 3, block_size, block_size), jnp.float32),
        jnp.zeros((tiles_here, points), jnp.float32),
    )
    local_terms, densities = lax.fori_loop(0, tiles_here, one_tile, start_carry)
    owner_part = lax.psum_scatter(
        local_terms.astype(jnp.bfloat16), "col", scatter_dimension=2, tiled=True
    ).astype(jnp.float32)
    mine = edge_rows(owner_part)
    xc_matrix = jnp.where(kept, jnp.pad(mine, ((0, 0), (1, 1), (0, 0), (0, 0))), 0.0)
    return (current, xc_matrix, densities)


BF16 = jnp.bfloat16
F32 = jnp.float32


def mixed(index, turn, count):
    return index ^ turn if count & (count - 1) == 0 else (turn - index) % count


class Chain:
    def __init__(self, rows, cols):
        self.rows, self.cols, self.count = rows, cols, rows * cols

    def device(self, block_row):
        pair, step = divmod(block_row, 2 * self.cols)
        plane, core = divmod(step, 2)
        plane = plane if pair % 2 == 0 else self.cols - 1 - plane
        return (2 * pair + core) * self.cols + plane

    def step(self, row_index, col_index):
        pair, core = row_index // 2, row_index % 2
        plane = jnp.where(pair % 2 == 0, col_index, self.cols - 1 - col_index)
        return 2 * plane + core

    def to_rows(self, turn):
        pairs = []
        for row in range(self.rows):
            for col in range(self.cols):
                pairs.append((row * self.cols + col, self.device(row * self.cols + mixed(col, turn, self.cols))))
        return pairs

    def to_slices(self, turn):
        return [(b, a) for a, b in self.to_rows(turn)]

    def shift(self, by):
        return [(self.device(i), self.device(i + by)) for i in range(self.count) if 0 <= i + by < self.count]


SMALL = 12 << 20
BOTH = ("row", "col")
VMEM_SPEC = pl.BlockSpec(memory_space=pltpu.VMEM)
SMEM_SPEC = pl.BlockSpec(memory_space=pltpu.SMEM)


def small_call(body, scalars, arrays, outs, scratch=()):
    return pl.pallas_call(
        body,
        in_specs=[SMEM_SPEC] * len(scalars) + [VMEM_SPEC] * len(arrays),
        out_specs=[VMEM_SPEC] * len(outs),
        out_shape=[jax.ShapeDtypeStruct(s, d) for s, d in outs],
        scratch_shapes=[pltpu.VMEM(s, d) for s, d in scratch],
        compiler_params=pltpu.CompilerParams(vmem_limit_bytes=SMALL),
    )(*scalars, *arrays)


HELD = (0, 2, 3)
SENDS = ((1, 5), (2, 5), (0, 4), (0, 3))
NOTE = 16


def grid_of(shape, axis):
    return lax.broadcasted_iota(jnp.int32, shape, axis)


def prepare(density, pattern, steps, slice_here):
    cols, _, high, block = density.shape
    tiles = steps.shape[0]

    def body(pattern_ref, steps_ref, slice_ref, density_ref, *outs):
        row, lane = grid_of((NOTE, block), 0), grid_of((NOTE, block), 1)
        for turn in range(cols):
            j = mixed(slice_ref[0], turn, cols)
            for k, d in enumerate(HELD):
                value = density_ref[j, d]
                outs[turn][k * high : (k + 1) * high] = jnp.where(pattern_ref[j, d] > 0, value, jnp.zeros_like(value))
            note = jnp.zeros((NOTE, block), F32)
            for d in range(5):
                note = jnp.where((row == 0) & (lane == d), (pattern_ref[j, d] > 0).astype(F32), note)
            for tile in range(tiles):
                note = jnp.where((row == 1) & (lane == tile), steps_ref[tile].astype(F32), note)
            outs[turn][3 * high :] = note.astype(BF16)

    shapes = [((3 * high + NOTE, block), BF16)] * cols
    return small_call(body, [pattern, steps, slice_here], [density], shapes)


def join_rows(pieces, place, block):
    cols = len(pieces)
    high = block // cols

    def body(place_ref, *refs):
        ins, (own, up, down, kept, steps) = refs[:cols], refs[cols:]
        row = grid_of((NOTE, block), 0)
        total = jnp.zeros((NOTE, block), F32)
        for turn in range(cols):
            source = mixed(place_ref[0], turn, cols)
            at = pl.ds(pl.multiple_of(source * high, high), high)
            for k in range(3):
                value = ins[turn][k * high : (k + 1) * high]
                own[k, at] = value
                if k > 0:
                    up[k - 1, at] = value
                if k < 2:
                    down[k, at] = value
            note = ins[turn][3 * high :].astype(F32)
            total = jnp.where(row == source, note[1:2], total)
        kept[...] = note
        steps[...] = total.astype(BF16)

    two, three = ((2, block, block), BF16), ((3, block, block), BF16)
    shapes = [three, two, two, ((NOTE, block), F32), ((NOTE, block), BF16)]
    return small_call(body, [place], pieces, shapes)


def exchange_rows(chain, sends):
    got = {}
    for by, send in zip((1, 2, -1, -2), sends):
        got[by] = lax.ppermute(send, BOTH, chain.shift(by))
    return got[1], got[2], got[-1], got[-2]


def purify_math(kept_ref, left, right, square, store):
    def product(left, d):
        far, total = d - 2, None
        for o in range(max(-2, far - 2), min(2, far + 2) + 1):
            term = jnp.dot(left(o), right(o, far), preferred_element_type=F32)
            total = term if total is None else total + term
        return jnp.where(kept_ref[0:1, d : d + 1] > 0.0, total, 0.0)

    for d in range(5):
        square[d] = product(left, d).astype(BF16)
    for d in range(5):
        value = 3.0 * square[d].astype(F32) - 2.0 * product(lambda o: square[o + 2], d)
        store(d, value.astype(BF16))


def purify_first(own, near, kept, block):
    places = [(a, b) for a in range(-2, 3) for b in range(-2, 3) if abs(a - b) <= 2]
    held = [(-2, -2), (-2, -1), (-1, -1), (-1, 0), (0, -2), (0, 0), (0, 1), (1, -1), (1, 1), (1, 2), (2, 0), (2, 2)]
    flipped = [(a, b) for a, b in places if (a, b) not in held]

    def body(kept_ref, own_ref, m1, m2, p1, p2, *refs):
        outs, (square, turned) = refs[:-2], refs[-2:]
        source = [(m2, 0), (m2, 1), (m1, 0), (m1, 1), (own_ref, 0), (own_ref, 1), (own_ref, 2)]
        source += [(p1, 0), (p1, 1), (p1, 2), (p2, 0), (p2, 1)]
        source = dict(zip(held, source))
        for k, (a, b) in enumerate(flipped):
            ref, at = source[b, a]
            turned[k] = ref[at].T
            source[a, b] = (turned, k)

        def block_at(a, b):
            ref, at = source[a, b]
            return ref[at]

        def store(d, value):
            outs[0][d] = value
            for out, (low, top) in zip(outs[1:], SENDS):
                if low <= d < top:
                    out[d - low] = value

        purify_math(kept_ref, lambda o: block_at(0, o), block_at, square, store)

    whole = ((5, block, block), BF16)
    shapes = [whole] + [((top - low, block, block), BF16) for low, top in SENDS]
    scratch = [whole, ((len(flipped), block, block), BF16)]
    return small_call(body, [], [kept, own] + list(near), shapes, scratch)


def purify_next(own, near, kept, block, place, steps, cols):
    high = block // cols
    last = place is not None

    def body(*refs):
        place_ref, refs = (refs[0], refs[1:]) if last else (None, refs)
        kept_ref, own_ref, m1, m2, p1, p2, steps_ref = refs[:7]
        outs, (square, whole_ref) = refs[7:-2], refs[-2:]

        def right(o, far):
            return (m2, m1, own_ref, p1, p2)[o + 2][far + (2, 2, 2, 1, 0)[o + 2]]

        def store(d, value):
            if last:
                whole_ref[d] = value
                return
            outs[0][d] = value
            for out, (low, top) in zip(outs[1:], SENDS):
                if low <= d < top:
                    out[d - low] = value

        purify_math(kept_ref, lambda o: own_ref[o + 2], right, square, store)
        if last:
            for turn in range(cols):
                at = pl.ds(pl.multiple_of(mixed(place_ref[0], turn, cols) * high, high), high)
                for d in range(5):
                    outs[turn][d * high : (d + 1) * high] = whole_ref[d, at]
                outs[turn][5 * high :] = steps_ref[...]

    whole = ((5, block, block), BF16)
    if last:
        shapes = [((5 * high + NOTE, block), BF16)] * cols
    else:
        shapes = [whole] + [((top - low, block, block), BF16) for low, top in SENDS]
    return small_call(body, [place] if last else [], [kept, own] + list(near) + [steps], shapes, [whole, whole])


def join_slices(pieces, place, block):
    cols = len(pieces)
    high = block // cols

    def body(place_ref, *refs):
        ins, (out, down, up) = refs[:cols], refs[cols:]
        for turn in range(cols):
            j = mixed(place_ref[0], turn, cols)
            for d in range(5):
                out[j, d] = ins[turn][d * high : (d + 1) * high]
        down[...] = out[cols - 1, 2:4]
        up[...] = out[0, 1:3]

    edge = ((2, high, block), BF16)
    return small_call(body, [place], pieces, [((cols, 5, high, block), BF16), edge, edge])


def read_steps(piece, cols, tiles):
    rows, block = piece.shape

    def body(piece_ref, steps):
        note = piece_ref[...].astype(F32)
        row, lane = grid_of((NOTE, block), 0), grid_of((NOTE, block), 1)
        for source in range(cols):
            for tile in range(tiles):
                here = jnp.where((row == source) & (lane == tile), note, 0.0)
                steps[source, tile] = jnp.sum(here).astype(jnp.int32)

    return pl.pallas_call(
        body,
        grid=(1,),
        in_specs=[pl.BlockSpec((NOTE, block), lambda i: (rows // NOTE - 1, 0))],
        out_specs=SMEM_SPEC,
        out_shape=jax.ShapeDtypeStruct((cols, tiles), jnp.int32),
        compiler_params=pltpu.CompilerParams(vmem_limit_bytes=1 << 20),
        name="read_steps",
    )(piece)


def slot_of(step, half):
    offset = step % 2
    first = (half - offset + 2) % 2
    return offset, first, (offset + first) // 2


def pack_windows(purified, above, below, steps, place, tiles, functions):
    cols, _, high, block = purified.shape
    part = functions // 3
    per_half = part // high

    def body(steps_ref, place_ref, pur, above_ref, below_ref, *refs):
        outs, near = refs[:-1], refs[-1]
        for low in range(2):
            for b in range(2):
                at = slice(b * block, (b + 1) * block)
                for row in range(cols + 2):
                    if low == 0 and row == 0:
                        near[low, row, :, at] = above_ref[b]
                    elif low == 1 and row == cols + 1:
                        near[low, row, :, at] = below_ref[b]
                    elif 0 < row < cols + 1:
                        near[low, row, :, at] = pur[row - 1, 2 - low + b]
        half = place_ref[0] // per_half
        for to in range(cols):
            for tile in range(tiles):
                step = steps_ref[to, tile]
                offset, _, low = slot_of(step, half)
                lanes = pl.ds(pl.multiple_of(offset * part, part), functions)
                outs[tile][to, 0] = near[low, step // 2 + low, :, lanes]
                outs[tile][to, 1] = near[1, step // 2 + 1, :, lanes]

    return small_call(
        body, [steps, place], [purified, above, below],
        [((cols, 2, high, functions), BF16)] * tiles, [((2, cols + 2, high, 2 * block), BF16)],
    )


def pointwise(n, g, w, points):
    u = n * n + 1.0
    a = jnp.exp(jnp.log(u) * (2.0 / 3.0))
    ia = 1.0 / a
    t = (g[0] * g[0] + g[1] * g[1] + g[2] * g[2]) * (ia * ia)
    part = 1.0 / (1.0 + (mu_pbe / kappa_pbe) * t)
    enhance = 1.0 + kappa_pbe - kappa_pbe * part
    slope = mu_pbe * part * part
    by_gradient = -slater_cx * slope * ia
    by_density = -slater_cx * a * (n / u) * ((4.0 / 3.0) * enhance - (8.0 / 3.0) * t * slope)
    scaled = w * (1.0 / points)
    return 0.5 * by_density * scaled, [2.0 * by_gradient * scaled * gk for gk in g]


def tile_call(tile, basis_values, basis_grads, weights, pieces, step, rows=1024, parts=2):
    tiles, points, functions = basis_values.shape
    cols, _, high, _ = pieces.shape
    part = functions // 3
    per_half = part // high
    count, sub, lanes = points // rows, rows // parts, functions // 128

    def body(step_ref, v_ref, g_ref, w_ref, pieces_ref, dens_ref, term_ref, win_ref, kept_ref, y_ref, *bufs):
        i = pl.program_id(0)
        offset = step_ref[0] % 2
        x_refs, z_refs = bufs[:parts], bufs[parts:]
        ones = jnp.ones((8, 128), BF16)

        @pl.when(i == 0)
        def _():
            kept_ref[...] = jnp.zeros(kept_ref.shape, BF16)
            z_refs[-1][...] = jnp.zeros(z_refs[-1].shape, BF16)
            y_ref[...] = jnp.zeros(y_ref.shape, F32)
            for h in range(3):
                for s in range(per_half):
                    source = per_half * ((offset + h) % 2) + s
                    win_ref[part * h + high * s : part * h + high * (s + 1)] = pieces_ref[source, h // 2]

        def columns(x):
            return [x[:, 128 * j : 128 * (j + 1)] for j in range(lanes)]

        def project(k):
            v = v_ref[sub * k : sub * (k + 1)]
            x_refs[k][...] = jnp.dot(v, win_ref[...], preferred_element_type=F32).astype(BF16)

        def row_sums(k):
            at = slice(sub * k, sub * (k + 1))
            x = columns(x_refs[k][...])

            def total(a):
                partial = sum(p * q for p, q in zip(x, columns(a)))
                return lax.dot_general(ones, partial, (((1,), (1,)), ((), ())), preferred_element_type=F32)

            return [total(v_ref[at])] + [total(g_ref[q, at]) for q in range(3)]

        def back(k):
            v = kept_ref[...] if k < 0 else v_ref[sub * k : sub * (k + 1)]
            y_ref[...] += lax.dot_general(
                v, z_refs[k][...], (((0,), (0,)), ((), ())), preferred_element_type=F32
            )

        def weigh(k, sums):
            at = slice(sub * k, sub * (k + 1))
            n = sums[0] * (1.0 / functions)
            g = [q * (2.0 / functions) for q in sums[1:]]
            dens_ref[:, at] = n[0:1]
            c0, ck = pointwise(n, g, jnp.broadcast_to(w_ref[tile : tile + 1, at], (8, sub)), points)
            factors = [c.astype(BF16) for c in [c0] + ck]
            for b in range(sub // 128):
                r = slice(sub * k + 128 * b, sub * k + 128 * (b + 1))
                f = [jnp.concatenate([c[:, 128 * b : 128 * (b + 1)]] * 16, axis=0).T for c in factors]
                arrays = [v_ref[r]] + [g_ref[q, r] for q in range(3)]
                for j in range(lanes):
                    t = [u * a[:, 128 * j : 128 * (j + 1)] for u, a in zip(f, arrays)]
                    z_refs[k][128 * b : 128 * (b + 1), 128 * j : 128 * (j + 1)] = (t[0] + t[1]) + (t[2] + t[3])

        project(0)
        for k in range(parts):
            if k + 1 < parts:
                project(k + 1)
            sums = row_sums(k)
            back(k - 1)
            weigh(k, sums)
        kept_ref[...] = v_ref[sub * (parts - 1) :]

        @pl.when(i == count - 1)
        def _():
            back(-1)
            y = y_ref[...]
            y_ref[...] = y + y.T
            for to in range(cols):
                _, first, _ = slot_of(step_ref[0], to // per_half)
                start = pl.multiple_of(part * first + high * (to % per_half), high)
                term_ref[to, 0] = y_ref[pl.ds(start, high)].astype(BF16)
                start = 2 * part + high * (to % per_half)
                term_ref[to, 1] = y_ref[start : start + high].astype(BF16)

    return pl.pallas_call(
        body,
        grid=(count,),
        in_specs=[
            SMEM_SPEC,
            pl.BlockSpec((None, rows, functions), lambda i: (tile, i, 0)),
            pl.BlockSpec((3, None, rows, functions), lambda i: (0, tile, i, 0)),
            pl.BlockSpec((tiles, rows), lambda i: (0, i)),
            VMEM_SPEC,
        ],
        out_specs=[pl.BlockSpec((1, rows), lambda i: (0, i)), VMEM_SPEC],
        out_shape=[
            jax.ShapeDtypeStruct((1, points), F32),
            jax.ShapeDtypeStruct(pieces.shape, BF16),
        ],
        scratch_shapes=[
            pltpu.VMEM((functions, functions), BF16),
            pltpu.VMEM((sub, functions), BF16),
            pltpu.VMEM((functions, functions), F32),
        ]
        + [pltpu.VMEM((sub, functions), BF16)] * (2 * parts),
        compiler_params=pltpu.CompilerParams(vmem_limit_bytes=48 << 20),
        name="tile",
    )(step, basis_values, basis_grads, weights, pieces)


def add_terms(terms, steps, place, block):
    tiles = len(terms)
    cols, _, high, functions = terms[0].shape
    part = functions // 3
    per_half = part // high

    def body(steps_ref, place_ref, *refs):
        ins, (own, to_above, to_below, total) = refs[:tiles], refs[tiles:]
        total[...] = jnp.zeros(total.shape, F32)
        half = place_ref[0] // per_half
        for source in range(cols):
            for tile in range(tiles):
                step = steps_ref[source, tile]
                offset, first, low = slot_of(step, half)
                lanes = pl.ds(pl.multiple_of(offset * part, part), functions)
                total[low, step // 2 + low, :, lanes] += ins[tile][source, 0].astype(F32)

                @pl.when(first == 0)
                def _():
                    total[1, step // 2 + 1, :, lanes] += ins[tile][source, 1].astype(F32)

        for row in range(1, cols + 1):
            own[row - 1, 0] = total[1, row, :, :block]
            own[row - 1, 1] = total[1, row, :, block:] + total[0, row, :, :block]
            own[row - 1, 2] = total[0, row, :, block:]
        for b in range(2):
            at = slice(b * block, (b + 1) * block)
            to_above[b] = total[0, 0, :, at].astype(BF16)
            to_below[b] = total[1, cols + 1, :, at].astype(BF16)

    edge = ((2, high, block), BF16)
    return small_call(
        body, [steps, place], list(terms),
        [((cols, 3, high, block), F32), edge, edge], [((2, cols + 2, high, 2 * block), F32)],
    )


def by_block_rows(density, pattern, windows, basis_values, basis_grads, weights):
    rows, cols = lax.axis_size("row"), lax.axis_size("col")
    row_index, col_index = lax.axis_index("row"), lax.axis_index("col")
    block = density.shape[3]
    tiles, _, functions = basis_values.shape
    chain = Chain(rows, cols)
    step_here = chain.step(row_index, col_index)
    place = (step_here % cols).astype(jnp.int32).reshape(1)
    slice_here = col_index.astype(jnp.int32).reshape(1)
    kept = (pattern > 0)[:, :, None, None]
    steps_here = (windows - (2 * cols * row_index - 2)).astype(jnp.int32)
    pieces = prepare(density, pattern, steps_here, slice_here)
    pieces = [lax.ppermute(p, BOTH, chain.to_rows(turn)) for turn, p in enumerate(pieces)]
    own, up, down, kept_row, steps = join_rows(pieces, place, block)
    sends = (up, up, own, down)
    for iteration in range(ITERS):
        near = exchange_rows(chain, sends)
        last = place if iteration == ITERS - 1 else None
        if iteration == 0:
            out = purify_first(own, near, kept_row, block)
        else:
            out = purify_next(own, near, kept_row, block, last, steps, cols)
        own, sends = out[0], out[1:]
    pieces = [lax.ppermute(p, BOTH, chain.to_slices(turn)) for turn, p in enumerate(out)]
    purified, down, up = join_slices(pieces, slice_here, block)
    steps = read_steps(pieces[0], cols, tiles)
    above = shifted_2(down, "row", 1)
    below = shifted_2(up, "row", -1)
    sent = pack_windows(purified, above, below, steps, slice_here, tiles, functions)

    densities, terms = [], []
    for tile in range(tiles):
        window = lax.all_to_all(sent[tile], "col", 0, 0, tiled=True)
        dens, term = tile_call(
            tile, basis_values, basis_grads, weights, window, steps_here[tile : tile + 1]
        )
        densities.append(dens)
        terms.append(lax.all_to_all(term, "col", 0, 0, tiled=True))
    mine, to_above, to_below = add_terms(terms, steps, slice_here, block)
    from_below = shifted_2(to_above, "row", -1).astype(F32)
    from_above = shifted_2(to_below, "row", 1).astype(F32)
    first = jnp.pad(from_above[None], ((0, cols - 1), (0, 1), (0, 0), (0, 0)))
    last = jnp.pad(from_below[None], ((cols - 1, 0), (1, 0), (0, 0), (0, 0)))
    summed = mine + first + last
    xc_matrix = jnp.where(kept, jnp.pad(summed, ((0, 0), (1, 1), (0, 0), (0, 0))), 0.0)
    return purified, xc_matrix, jnp.concatenate(densities)


def on_device(density, pattern, windows, basis_values, basis_grads, weights):
    rows, cols = lax.axis_size("row"), lax.axis_size("col")
    band_rows, block, functions = density.shape[0], density.shape[3], basis_values.shape[2]
    fits = (
        band_rows == cols
        and rows % 2 == 0
        and 2 * functions == 3 * block
        and functions // 3 % density.shape[2] == 0
        and cols <= NOTE
        and (5 * density.shape[2]) % NOTE == 0
        and 2 * cols + 2 <= 256
        and basis_values.shape[1] % 1024 == 0
    )
    plan = by_block_rows if fits else by_gathers
    return plan(density, pattern, windows, basis_values, basis_grads, weights)


def solution(mesh):
    placed = (
        P("row", None, "col", None),
        P("row", None),
        P(("row", "col")),
        P(("row", "col"), None, None),
        P(None, ("row", "col"), None, None),
        P(("row", "col"), None),
    )
    return jax.shard_map(
        on_device,
        mesh=mesh,
        in_specs=placed,
        out_specs=(
            P("row", None, "col", None),
            P("row", None, "col", None),
            P(("row", "col"), None),
        ),
        check_vma=False,
    )
```

```python
import jax
import jax.numpy as jnp
from jax import lax
from jax.experimental import pallas as pl
from jax.experimental.pallas import tpu as pltpu
from jax.sharding import PartitionSpec as P

ITERS = 2


slater_cx = 0.7386
kappa_pbe = 0.804
mu_pbe = 0.2195


def padded(cells, sides, width):
    for axis, dim in sides:
        count = lax.axis_size(axis)
        ends = count - 1
        head = lax.slice_in_dim(cells, 0, width, axis=dim)
        tail = lax.slice_in_dim(cells, cells.shape[dim] - width, cells.shape[dim], axis=dim)
        cells = jnp.concatenate(
            [
                lax.ppermute(tail, axis, [(i, (i + 1) % count) for i in range(ends)]),
                cells,
                lax.ppermute(head, axis, [((i + 1) % count, i) for i in range(ends)]),
            ],
            axis=dim,
        )
    return cells


def shifted_2(value, axis, by):
    length = lax.axis_size(axis)
    pairs = [(i, i + by) for i in range(length) if 0 <= i + by < length]
    return lax.ppermute(value, axis, pairs)


def energy_sum(point_density, grad_square):
    spread = jnp.sqrt(point_density * point_density + 1.0)
    reduced = grad_square / spread ** (8.0 / 3.0)
    enhance = 1.0 + kappa_pbe - kappa_pbe / (1.0 + mu_pbe * reduced / kappa_pbe)
    return jnp.sum(-slater_cx * spread ** (4.0 / 3.0) * enhance)


def tile_terms(values, grads, quadrature, window_block):
    functions = values.shape[1]
    points = values.shape[0]
    projected = jnp.dot(values, window_block, preferred_element_type=jnp.float32)
    point_density = jnp.sum(projected * values.astype(jnp.float32), axis=1) / functions
    slopes = 2.0 * jnp.sum(projected[None] * grads.astype(jnp.float32), axis=2) / functions
    grad_square = jnp.sum(slopes * slopes, axis=0)
    by_density, by_gradient = jax.grad(energy_sum, argnums=(0, 1))(point_density, grad_square)
    scaled = quadrature / points
    weighted = (0.5 * by_density * scaled)[:, None] * values.astype(jnp.float32)
    weighted = weighted + jnp.sum(
        ((2.0 * by_gradient * scaled)[None] * slopes)[:, :, None] * grads.astype(jnp.float32),
        axis=0,
    )
    weighted = weighted.astype(jnp.bfloat16)
    one_side = lax.dot_general(
        values, weighted, (((0,), (0,)), ((), ())), preferred_element_type=jnp.float32
    )
    return (point_density, one_side + one_side.T)


def band_product(left, right_padded):
    blocks = left.shape[0]
    total = None
    for offset_step in range(5):
        shifted = right_padded[offset_step : offset_step + blocks]
        widened = jnp.pad(shifted, ((0, 0), (2, 2), (0, 0), (0, 0)))
        picked = widened[:, 4 - offset_step : 9 - offset_step]
        term = jnp.einsum(
            "brk,bdkc->bdrc", left[:, offset_step], picked, preferred_element_type=jnp.float32
        )
        total = term if total is None else total + term
    return total


def window_of(band_three, lead, offset, functions):
    paired = lax.dynamic_slice_in_dim(band_three, lead, 2, 0)
    upper = jnp.concatenate([paired[0, 1], paired[0, 2]], axis=1)
    lower = jnp.concatenate([paired[1, 0], paired[1, 1]], axis=1)
    dense = jnp.concatenate([upper, lower], axis=0)
    return lax.dynamic_slice(dense, (offset, offset), (functions, functions))


def spread_term(summed, term, lead, offset):
    width = summed.shape[2]
    dense = lax.dynamic_update_slice(
        jnp.zeros((2 * width, 2 * width), summed.dtype), term, (offset, offset)
    )
    nothing = jnp.zeros((width, width), summed.dtype)
    upper = jnp.stack([nothing, dense[:width, :width], dense[:width, width:]])
    lower = jnp.stack([dense[width:, :width], dense[width:, width:], nothing])
    increment = jnp.stack([upper, lower])
    paired = lax.dynamic_slice_in_dim(summed, lead, 2, 0)
    return lax.dynamic_update_slice_in_dim(summed, paired + increment, lead, 0)


def times_current(left, current):
    near_right = padded(current, (("row", 0),), 2)
    return band_product(left, lax.all_gather(near_right, "col", axis=2, tiled=True))


def edge_rows(summed):
    blocks = summed.shape[0] - 2
    from_above = shifted_2(summed[0].astype(jnp.bfloat16), "row", -1).astype(jnp.float32)
    from_below = shifted_2(summed[blocks + 1].astype(jnp.bfloat16), "row", 1).astype(jnp.float32)
    own_rows = summed[1 : blocks + 1]
    return jnp.concatenate(
        [
            own_rows[:1] + from_below[None],
            own_rows[1 : blocks - 1],
            own_rows[blocks - 1 :] + from_above[None],
        ],
        axis=0,
    )


def by_gathers(density, pattern, windows, basis_values, basis_grads, weights):
    row_index = lax.axis_index("row")
    band_rows = density.shape[0]
    functions = basis_values.shape[2]
    step_size = functions // 3
    kept = (pattern > 0)[:, :, None, None]
    current = jnp.where(kept, density, jnp.zeros_like(density))
    for _ in range(ITERS):
        square = jnp.where(kept, times_current(current, current), 0.0).astype(jnp.bfloat16)
        cubic = times_current(square, current)
        current = jnp.where(kept, 3.0 * square.astype(jnp.float32) - 2.0 * cubic, 0.0).astype(
            jnp.bfloat16
        )
    rows_full = lax.all_gather(current, "col", axis=2, tiled=True)
    near_full = padded(rows_full, (("row", 0),), 1)
    near = near_full[:, 1:4]
    tiles_here = windows.shape[0]
    points = basis_values.shape[1]
    block_size = near.shape[2]

    def one_tile(tile_index, carry):
        summed, densities = carry
        position = tile_index.astype(jnp.int32)
        start_step = windows[position]
        lead = start_step // 2 - (band_rows * row_index - 1)
        offset = start_step % 2 * step_size
        window_block = window_of(near, lead, offset, functions)
        values = lax.dynamic_index_in_dim(basis_values, position, 0, keepdims=False)
        grads = lax.dynamic_index_in_dim(basis_grads, position, 1, keepdims=False)
        quadrature = lax.dynamic_index_in_dim(weights, position, 0, keepdims=False)
        point_density, contribution = tile_terms(values, grads, quadrature, window_block)
        summed = spread_term(summed, contribution, lead, offset)
        densities = lax.dynamic_update_index_in_dim(densities, point_density, position, 0)
        return (summed, densities)

    start_carry = (
        jnp.zeros((band_rows + 2, 3, block_size, block_size), jnp.float32),
        jnp.zeros((tiles_here, points), jnp.float32),
    )
    local_terms, densities = lax.fori_loop(0, tiles_here, one_tile, start_carry)
    owner_part = lax.psum_scatter(
        local_terms.astype(jnp.bfloat16), "col", scatter_dimension=2, tiled=True
    ).astype(jnp.float32)
    mine = edge_rows(owner_part)
    xc_matrix = jnp.where(kept, jnp.pad(mine, ((0, 0), (1, 1), (0, 0), (0, 0))), 0.0)
    return (current, xc_matrix, densities)


BF16 = jnp.bfloat16
F32 = jnp.float32


def mixed(index, turn, count):
    return index ^ turn if count & (count - 1) == 0 else (turn - index) % count


class Chain:
    def __init__(self, rows, cols):
        self.rows, self.cols, self.count = rows, cols, rows * cols

    def device(self, block_row):
        pair, step = divmod(block_row, 2 * self.cols)
        plane, core = divmod(step, 2)
        plane = plane if pair % 2 == 0 else self.cols - 1 - plane
        return (2 * pair + core) * self.cols + plane

    def step(self, row_index, col_index):
        pair, core = row_index // 2, row_index % 2
        plane = jnp.where(pair % 2 == 0, col_index, self.cols - 1 - col_index)
        return 2 * plane + core

    def to_rows(self, turn):
        pairs = []
        for row in range(self.rows):
            for col in range(self.cols):
                pairs.append((row * self.cols + col, self.device(row * self.cols + mixed(col, turn, self.cols))))
        return pairs

    def to_slices(self, turn):
        return [(b, a) for a, b in self.to_rows(turn)]

    def edges(self, turn):
        pairs, other = [], (turn + self.cols // 2) % self.cols
        for row in range(self.rows):
            if row + 1 < self.rows:
                pairs.append((self.device((row + 1) * self.cols - 1), (row + 1) * self.cols + turn))
            if row > 0:
                pairs.append((self.device(row * self.cols), (row - 1) * self.cols + other))
        return pairs

    def shift(self, by):
        return [(self.device(i), self.device(i + by)) for i in range(self.count) if 0 <= i + by < self.count]


SMALL = 12 << 20
LARGE = 60 << 20
BOTH = ("row", "col")
VMEM_SPEC = pl.BlockSpec(memory_space=pltpu.VMEM)
SMEM_SPEC = pl.BlockSpec(memory_space=pltpu.SMEM)


def with_ids(body, before):
    def wrapped(*refs):
        ids = [ref[0] for ref in refs[before : before + 3]]
        return body(*refs[:before], ids, *refs[before + 3 :])

    return wrapped


def small_call(body, scalars, arrays, outs, scratch=(), limit=SMALL):
    return pl.pallas_call(
        with_ids(body, len(scalars) - 3) if len(scalars) >= 3 else body,
        in_specs=[SMEM_SPEC] * len(scalars) + [VMEM_SPEC] * len(arrays),
        out_specs=[VMEM_SPEC] * len(outs),
        out_shape=[jax.ShapeDtypeStruct(s, d) for s, d in outs],
        scratch_shapes=[pltpu.VMEM(s, d) for s, d in scratch],
        compiler_params=pltpu.CompilerParams(vmem_limit_bytes=limit),
    )(*scalars, *arrays)


HELD = (0, 2, 3)
SENDS = ((1, 5), (2, 5), (0, 4), (0, 3))
NOTE = 16
PLACE, SLICE, BASE = range(3)


def grid_of(shape, axis):
    return lax.broadcasted_iota(jnp.int32, shape, axis)


def prepare(density, pattern, windows, ids):
    cols, _, high, block = density.shape
    tiles = windows.shape[0]

    def body(pattern_ref, windows_ref, ids, density_ref, *outs):
        row, lane = grid_of((NOTE, block), 0), grid_of((NOTE, block), 1)
        for turn in range(cols):
            j = mixed(ids[SLICE], turn, cols)
            for k, d in enumerate(HELD):
                value = density_ref[j, d]
                outs[turn][k * high : (k + 1) * high] = jnp.where(pattern_ref[j, d] > 0, value, jnp.zeros_like(value))
            note = jnp.zeros((NOTE, block), F32)
            for d in range(5):
                note = jnp.where((row == 0) & (lane == d), (pattern_ref[j, d] > 0).astype(F32), note)
            for tile in range(tiles):
                note = jnp.where((row == 1) & (lane == tile), (windows_ref[tile] - ids[BASE]).astype(F32), note)
            outs[turn][3 * high :] = note.astype(BF16)

    shapes = [((3 * high + NOTE, block), BF16)] * cols
    return small_call(body, [pattern, windows, *ids], [density], shapes, limit=LARGE)


def join_rows(pieces, place, block):
    cols = len(pieces)
    high = block // cols

    def body(ids, *refs):
        ins, (own, up, down, kept, steps) = refs[:cols], refs[cols:]
        row = grid_of((NOTE, block), 0)
        total = jnp.zeros((NOTE, block), F32)
        for turn in range(cols):
            source = mixed(ids[PLACE], turn, cols)
            at = pl.ds(pl.multiple_of(source * high, high), high)
            for k in range(3):
                value = ins[turn][k * high : (k + 1) * high]
                own[k, at] = value
                if k > 0:
                    up[k - 1, at] = value
                if k < 2:
                    down[k, at] = value
            note = ins[turn][3 * high :].astype(F32)
            total = jnp.where(row == source, note[1:2], total)
        kept[...] = note
        steps[...] = total.astype(BF16)

    two, three = ((2, block, block), BF16), ((3, block, block), BF16)
    shapes = [three, two, two, ((NOTE, block), F32), ((NOTE, block), BF16)]
    return small_call(body, place, pieces, shapes)


def exchange_rows(chain, sends):
    got = {}
    for by, send in zip((1, 2, -1, -2), sends):
        got[by] = lax.ppermute(send, BOTH, chain.shift(by))
    return got[1], got[2], got[-1], got[-2]


def purify_math(kept_ref, left, right, square, store):
    def product(left, d):
        far, total = d - 2, None
        for o in range(max(-2, far - 2), min(2, far + 2) + 1):
            term = jnp.dot(left(o), right(o, far), preferred_element_type=F32)
            total = term if total is None else total + term
        return jnp.where(kept_ref[0:1, d : d + 1] > 0.0, total, 0.0)

    for d in range(5):
        square[d] = product(left, d).astype(BF16)
    for d in range(5):
        value = 3.0 * square[d].astype(F32) - 2.0 * product(lambda o: square[o + 2], d)
        store(d, value.astype(BF16))


def purify_first(own, near, kept, block):
    places = [(a, b) for a in range(-2, 3) for b in range(-2, 3) if abs(a - b) <= 2]
    held = [(-2, -2), (-2, -1), (-1, -1), (-1, 0), (0, -2), (0, 0), (0, 1), (1, -1), (1, 1), (1, 2), (2, 0), (2, 2)]
    flipped = [(a, b) for a, b in places if (a, b) not in held]

    def body(kept_ref, own_ref, m1, m2, p1, p2, *refs):
        outs, (square, turned) = refs[:-2], refs[-2:]
        source = [(m2, 0), (m2, 1), (m1, 0), (m1, 1), (own_ref, 0), (own_ref, 1), (own_ref, 2)]
        source += [(p1, 0), (p1, 1), (p1, 2), (p2, 0), (p2, 1)]
        source = dict(zip(held, source))
        for k, (a, b) in enumerate(flipped):
            ref, at = source[b, a]
            turned[k] = ref[at].T
            source[a, b] = (turned, k)

        def block_at(a, b):
            ref, at = source[a, b]
            return ref[at]

        def store(d, value):
            outs[0][d] = value
            for out, (low, top) in zip(outs[1:], SENDS):
                if low <= d < top:
                    out[d - low] = value

        purify_math(kept_ref, lambda o: block_at(0, o), block_at, square, store)

    whole = ((5, block, block), BF16)
    shapes = [whole] + [((top - low, block, block), BF16) for low, top in SENDS]
    scratch = [whole, ((len(flipped), block, block), BF16)]
    return small_call(body, [], [kept, own] + list(near), shapes, scratch)


def purify_next(own, near, kept, block, place, steps, cols):
    high = block // cols
    last = place is not None

    def body(*refs):
        ids, refs = (refs[0], refs[1:]) if last else (None, refs)
        kept_ref, own_ref, m1, m2, p1, p2, steps_ref = refs[:7]
        outs, (square, whole_ref) = refs[7:-2], refs[-2:]

        def right(o, far):
            return (m2, m1, own_ref, p1, p2)[o + 2][far + (2, 2, 2, 1, 0)[o + 2]]

        def store(d, value):
            if last:
                whole_ref[d] = value
                return
            outs[0][d] = value
            for out, (low, top) in zip(outs[1:], SENDS):
                if low <= d < top:
                    out[d - low] = value

        purify_math(kept_ref, lambda o: own_ref[o + 2], right, square, store)
        if last:
            for turn in range(cols):
                at = pl.ds(pl.multiple_of(mixed(ids[PLACE], turn, cols) * high, high), high)
                for d in range(5):
                    outs[turn][d * high : (d + 1) * high] = whole_ref[d, at]
                outs[turn][5 * high :] = steps_ref[...]

                @pl.when(ids[PLACE] == cols - 1)
                def _():
                    outs[cols + turn][...] = whole_ref[2:4, high * turn : high * (turn + 1)]

                @pl.when(ids[PLACE] == 0)
                def _():
                    other = (turn + cols // 2) % cols
                    outs[cols + turn][...] = whole_ref[1:3, high * other : high * (other + 1)]

    whole = ((5, block, block), BF16)
    if last:
        shapes = [((5 * high + NOTE, block), BF16)] * cols + [((2, high, block), BF16)] * cols
    else:
        shapes = [whole] + [((top - low, block, block), BF16) for low, top in SENDS]
    return small_call(body, place if last else [], [kept, own] + list(near) + [steps], shapes, [whole, whole])


def join_slices(pieces, ids, block, after):
    cols = len(pieces)
    high = block // cols

    def body(ids, *refs):
        ins, out = refs[:cols], refs[-1]
        for turn in range(cols):
            j = mixed(ids[SLICE], turn, cols)
            for d in range(5):
                out[j, d] = ins[turn][d * high : (d + 1) * high]

    return pl.pallas_call(
        with_ids(body, 0),
        in_specs=[SMEM_SPEC] * 3 + [VMEM_SPEC] * cols + [pl.BlockSpec(memory_space=pl.ANY)],
        out_specs=VMEM_SPEC,
        out_shape=jax.ShapeDtypeStruct((cols, 5, high, block), BF16),
        compiler_params=pltpu.CompilerParams(vmem_limit_bytes=SMALL),
        name="join_slices",
    )(*ids, *pieces, after)


def read_steps(piece, cols, tiles):
    rows, block = piece.shape

    def body(piece_ref, steps):
        note = piece_ref[...].astype(F32)
        row, lane = grid_of((NOTE, block), 0), grid_of((NOTE, block), 1)
        for source in range(cols):
            for tile in range(tiles):
                here = jnp.where((row == source) & (lane == tile), note, 0.0)
                steps[source, tile] = jnp.sum(here).astype(jnp.int32)

    return pl.pallas_call(
        body,
        grid=(1,),
        in_specs=[pl.BlockSpec((NOTE, block), lambda i: (rows // NOTE - 1, 0))],
        out_specs=SMEM_SPEC,
        out_shape=jax.ShapeDtypeStruct((cols, tiles), jnp.int32),
        compiler_params=pltpu.CompilerParams(vmem_limit_bytes=1 << 20),
        name="read_steps",
    )(piece)


def slot_of(step, half):
    offset = step % 2
    first = (half - offset + 2) % 2
    return offset, first, (offset + first) // 2


def pack_windows(pieces, edges, steps, ids, block, tiles, functions):
    cols = len(pieces)
    high = block // cols
    part = functions // 3
    per_half = part // high

    def body(steps_ref, ids, *refs):
        ins, edge_ins, outs, near = refs[:cols], refs[cols : 2 * cols], refs[2 * cols : -1], refs[-1]
        here = ids[SLICE]
        for turn in range(cols):
            row = mixed(here, turn, cols) + 1
            for low in range(2):
                for b in range(2):
                    d = 2 - low + b
                    near[low, row, :, b * block : (b + 1) * block] = ins[turn][d * high : (d + 1) * high]

            @pl.when(here == turn)
            def _():
                for b in range(2):
                    near[0, 0, :, b * block : (b + 1) * block] = edge_ins[turn][b]

            @pl.when(here == (turn + cols // 2) % cols)
            def _():
                for b in range(2):
                    near[1, cols + 1, :, b * block : (b + 1) * block] = edge_ins[turn][b]

        half = here // per_half
        for to in range(cols):
            for tile in range(tiles):
                step = steps_ref[to, tile]
                offset, _, low = slot_of(step, half)
                lanes = pl.ds(pl.multiple_of(offset * part, part), functions)
                outs[tile][to, 0] = near[low, step // 2 + low, :, lanes]
                outs[tile][to, 1] = near[1, step // 2 + 1, :, lanes]

    return small_call(
        body, [steps, *ids], list(pieces) + list(edges),
        [((cols, 2, high, functions), BF16)] * tiles, [((2, cols + 2, high, 2 * block), BF16)],
    )


def pointwise(n, g, w, points):
    u = n * n + 1.0
    a = jnp.exp(jnp.log(u) * (2.0 / 3.0))
    ia = 1.0 / a
    t = (g[0] * g[0] + g[1] * g[1] + g[2] * g[2]) * (ia * ia)
    part = 1.0 / (1.0 + (mu_pbe / kappa_pbe) * t)
    enhance = 1.0 + kappa_pbe - kappa_pbe * part
    slope = mu_pbe * part * part
    by_gradient = -slater_cx * slope * ia
    by_density = -slater_cx * a * (n / u) * ((4.0 / 3.0) * enhance - (8.0 / 3.0) * t * slope)
    scaled = w * (1.0 / points)
    return 0.5 * by_density * scaled, [2.0 * by_gradient * scaled * gk for gk in g]


def tile_call(tile, basis_values, basis_grads, weights, pieces, windows, ids, rows=1024, parts=2):
    tiles, points, functions = basis_values.shape
    cols, _, high, _ = pieces.shape
    part = functions // 3
    per_half = part // high
    count, sub, lanes = points // rows, rows // parts, functions // 128

    def body(windows_ref, ids, v_ref, g_ref, w_ref, pieces_ref, dens_ref, term_ref, win_ref, kept_ref, y_ref, *bufs):
        i = pl.program_id(0)
        step = windows_ref[tile] - ids[BASE]
        offset = step % 2
        x_refs, z_refs = bufs[:parts], bufs[parts:]
        ones = jnp.ones((8, 128), BF16)

        @pl.when(i == 0)
        def _():
            kept_ref[...] = jnp.zeros(kept_ref.shape, BF16)
            z_refs[-1][...] = jnp.zeros(z_refs[-1].shape, BF16)
            y_ref[...] = jnp.zeros(y_ref.shape, F32)
            for h in range(3):
                for s in range(per_half):
                    source = per_half * ((offset + h) % 2) + s
                    win_ref[part * h + high * s : part * h + high * (s + 1)] = pieces_ref[source, h // 2]

        def columns(x):
            return [x[:, 128 * j : 128 * (j + 1)] for j in range(lanes)]

        def project(k):
            v = v_ref[sub * k : sub * (k + 1)]
            x_refs[k][...] = jnp.dot(v, win_ref[...], preferred_element_type=F32).astype(BF16)

        def row_sums(k):
            at = slice(sub * k, sub * (k + 1))
            x = columns(x_refs[k][...])

            def total(a):
                partial = sum(p * q for p, q in zip(x, columns(a)))
                return lax.dot_general(ones, partial, (((1,), (1,)), ((), ())), preferred_element_type=F32)

            return [total(v_ref[at])] + [total(g_ref[q, at]) for q in range(3)]

        def back(k):
            v = kept_ref[...] if k < 0 else v_ref[sub * k : sub * (k + 1)]
            y_ref[...] += lax.dot_general(
                v, z_refs[k][...], (((0,), (0,)), ((), ())), preferred_element_type=F32
            )

        def weigh(k, sums):
            at = slice(sub * k, sub * (k + 1))
            n = sums[0] * (1.0 / functions)
            g = [q * (2.0 / functions) for q in sums[1:]]
            dens_ref[:, at] = n[0:1]
            c0, ck = pointwise(n, g, jnp.broadcast_to(w_ref[tile : tile + 1, at], (8, sub)), points)
            factors = [c.astype(BF16) for c in [c0] + ck]
            for b in range(sub // 128):
                r = slice(sub * k + 128 * b, sub * k + 128 * (b + 1))
                f = [jnp.concatenate([c[:, 128 * b : 128 * (b + 1)]] * 16, axis=0).T for c in factors]
                arrays = [v_ref[r]] + [g_ref[q, r] for q in range(3)]
                for j in range(lanes):
                    t = [u * a[:, 128 * j : 128 * (j + 1)] for u, a in zip(f, arrays)]
                    z_refs[k][128 * b : 128 * (b + 1), 128 * j : 128 * (j + 1)] = (t[0] + t[1]) + (t[2] + t[3])

        project(0)
        for k in range(parts):
            if k + 1 < parts:
                project(k + 1)
            sums = row_sums(k)
            back(k - 1)
            weigh(k, sums)
        kept_ref[...] = v_ref[sub * (parts - 1) :]

        @pl.when(i == count - 1)
        def _():
            back(-1)
            y = y_ref[...]
            y_ref[...] = y + y.T
            for to in range(cols):
                _, first, _ = slot_of(step, to // per_half)
                start = pl.multiple_of(part * first + high * (to % per_half), high)
                term_ref[to, 0] = y_ref[pl.ds(start, high)].astype(BF16)
                start = 2 * part + high * (to % per_half)
                term_ref[to, 1] = y_ref[start : start + high].astype(BF16)

    return pl.pallas_call(
        with_ids(body, 1),
        grid=(count,),
        in_specs=[
            SMEM_SPEC,
            SMEM_SPEC,
            SMEM_SPEC,
            SMEM_SPEC,
            pl.BlockSpec((None, rows, functions), lambda i: (tile, i, 0)),
            pl.BlockSpec((3, None, rows, functions), lambda i: (0, tile, i, 0)),
            pl.BlockSpec((tiles, rows), lambda i: (0, i)),
            VMEM_SPEC,
        ],
        out_specs=[pl.BlockSpec((1, rows), lambda i: (0, i)), VMEM_SPEC],
        out_shape=[
            jax.ShapeDtypeStruct((1, points), F32),
            jax.ShapeDtypeStruct(pieces.shape, BF16),
        ],
        scratch_shapes=[
            pltpu.VMEM((functions, functions), BF16),
            pltpu.VMEM((sub, functions), BF16),
            pltpu.VMEM((functions, functions), F32),
        ]
        + [pltpu.VMEM((sub, functions), BF16)] * (2 * parts),
        compiler_params=pltpu.CompilerParams(vmem_limit_bytes=48 << 20),
        name="tile",
    )(windows, *ids, basis_values, basis_grads, weights, pieces)


def add_terms(terms, steps, place, block):
    tiles = len(terms)
    cols, _, high, functions = terms[0].shape
    part = functions // 3
    per_half = part // high

    def body(steps_ref, ids, *refs):
        ins, (own, to_above, to_below, total) = refs[:tiles], refs[tiles:]
        total[...] = jnp.zeros(total.shape, F32)
        half = ids[SLICE] // per_half
        for source in range(cols):
            for tile in range(tiles):
                step = steps_ref[source, tile]
                offset, first, low = slot_of(step, half)
                lanes = pl.ds(pl.multiple_of(offset * part, part), functions)
                total[low, step // 2 + low, :, lanes] += ins[tile][source, 0].astype(F32)

                @pl.when(first == 0)
                def _():
                    total[1, step // 2 + 1, :, lanes] += ins[tile][source, 1].astype(F32)

        for row in range(1, cols + 1):
            own[row - 1, 0] = total[1, row, :, :block]
            own[row - 1, 1] = total[1, row, :, block:] + total[0, row, :, :block]
            own[row - 1, 2] = total[0, row, :, block:]
        for b in range(2):
            at = slice(b * block, (b + 1) * block)
            to_above[b] = total[0, 0, :, at].astype(BF16)
            to_below[b] = total[1, cols + 1, :, at].astype(BF16)

    edge = ((2, high, block), BF16)
    return small_call(
        body, [steps, *place], list(terms),
        [((cols, 3, high, block), F32), edge, edge], [((2, cols + 2, high, 2 * block), F32)],
    )


def by_block_rows(density, pattern, windows, basis_values, basis_grads, weights):
    rows, cols = lax.axis_size("row"), lax.axis_size("col")
    row_index, col_index = lax.axis_index("row"), lax.axis_index("col")
    block = density.shape[3]
    tiles, _, functions = basis_values.shape
    chain = Chain(rows, cols)
    place = chain.step(row_index, col_index) % cols
    ids = [x.astype(jnp.int32).reshape(1) for x in (place, col_index, 2 * cols * row_index - 2)]
    pieces = prepare(density, pattern, windows, ids)
    pieces = [lax.ppermute(p, BOTH, chain.to_rows(turn)) for turn, p in enumerate(pieces)]
    own, up, down, kept_row, steps = join_rows(pieces, ids, block)
    sends = (up, up, own, down)
    for iteration in range(ITERS):
        near = exchange_rows(chain, sends)
        if iteration == 0:
            out = purify_first(own, near, kept_row, block)
        else:
            out = purify_next(own, near, kept_row, block, ids if iteration == ITERS - 1 else None, steps, cols)
        own, sends = out[0], out[1:]
    pieces, edges = [], []
    for turn in range(cols):
        pieces.append(lax.ppermute(out[turn], BOTH, chain.to_slices(turn)))
    for turn in range(cols):
        edges.append(lax.ppermute(out[cols + turn], BOTH, chain.edges(turn)))
    steps = read_steps(pieces[0], cols, tiles)
    sent = pack_windows(pieces, edges, steps, ids, block, tiles, functions)
    purified = join_slices(pieces, ids, block, sent[0])

    densities, terms = [], []
    for tile in range(tiles):
        window = lax.all_to_all(sent[tile], "col", 0, 0, tiled=True)
        dens, term = tile_call(tile, basis_values, basis_grads, weights, window, windows, ids)
        densities.append(dens)
        terms.append(lax.all_to_all(term, "col", 0, 0, tiled=True))
    mine, to_above, to_below = add_terms(terms, steps, ids, block)
    from_below = shifted_2(to_above, "row", -1).astype(F32)
    from_above = shifted_2(to_below, "row", 1).astype(F32)
    first = jnp.pad(from_above[None], ((0, cols - 1), (0, 1), (0, 0), (0, 0)))
    last = jnp.pad(from_below[None], ((cols - 1, 0), (1, 0), (0, 0), (0, 0)))
    summed = jnp.pad(mine + first + last, ((0, 0), (1, 1), (0, 0), (0, 0)))
    xc_matrix = jnp.where((pattern > 0)[:, :, None, None], summed, 0.0)
    return purified, xc_matrix, jnp.concatenate(densities)


def on_device(density, pattern, windows, basis_values, basis_grads, weights):
    rows, cols = lax.axis_size("row"), lax.axis_size("col")
    band_rows, block, functions = density.shape[0], density.shape[3], basis_values.shape[2]
    fits = (
        band_rows == cols
        and rows % 2 == 0
        and cols > 1
        and 2 * functions == 3 * block
        and functions // 3 % density.shape[2] == 0
        and cols <= NOTE
        and (5 * density.shape[2]) % NOTE == 0
        and 2 * cols + 2 <= 256
        and basis_values.shape[1] % 1024 == 0
    )
    plan = by_block_rows if fits else by_gathers
    return plan(density, pattern, windows, basis_values, basis_grads, weights)


def solution(mesh):
    placed = (
        P("row", None, "col", None),
        P("row", None),
        P(("row", "col")),
        P(("row", "col"), None, None),
        P(None, ("row", "col"), None, None),
        P(("row", "col"), None),
    )
    return jax.shard_map(
        on_device,
        mesh=mesh,
        in_specs=placed,
        out_specs=(
            P("row", None, "col", None),
            P("row", None, "col", None),
            P(("row", "col"), None),
        ),
        check_vma=False,
    )
```

```python
import jax
import jax.numpy as jnp
from jax import lax
from jax.experimental import pallas as pl
from jax.experimental.pallas import tpu as pltpu
from jax.sharding import PartitionSpec as P

ITERS = 2


slater_cx = 0.7386
kappa_pbe = 0.804
mu_pbe = 0.2195


def padded(cells, sides, width):
    for axis, dim in sides:
        count = lax.axis_size(axis)
        ends = count - 1
        head = lax.slice_in_dim(cells, 0, width, axis=dim)
        tail = lax.slice_in_dim(cells, cells.shape[dim] - width, cells.shape[dim], axis=dim)
        cells = jnp.concatenate(
            [
                lax.ppermute(tail, axis, [(i, (i + 1) % count) for i in range(ends)]),
                cells,
                lax.ppermute(head, axis, [((i + 1) % count, i) for i in range(ends)]),
            ],
            axis=dim,
        )
    return cells


def shifted_2(value, axis, by):
    length = lax.axis_size(axis)
    pairs = [(i, i + by) for i in range(length) if 0 <= i + by < length]
    return lax.ppermute(value, axis, pairs)


def energy_sum(point_density, grad_square):
    spread = jnp.sqrt(point_density * point_density + 1.0)
    reduced = grad_square / spread ** (8.0 / 3.0)
    enhance = 1.0 + kappa_pbe - kappa_pbe / (1.0 + mu_pbe * reduced / kappa_pbe)
    return jnp.sum(-slater_cx * spread ** (4.0 / 3.0) * enhance)


def tile_terms(values, grads, quadrature, window_block):
    functions = values.shape[1]
    points = values.shape[0]
    projected = jnp.dot(values, window_block, preferred_element_type=jnp.float32)
    point_density = jnp.sum(projected * values.astype(jnp.float32), axis=1) / functions
    slopes = 2.0 * jnp.sum(projected[None] * grads.astype(jnp.float32), axis=2) / functions
    grad_square = jnp.sum(slopes * slopes, axis=0)
    by_density, by_gradient = jax.grad(energy_sum, argnums=(0, 1))(point_density, grad_square)
    scaled = quadrature / points
    weighted = (0.5 * by_density * scaled)[:, None] * values.astype(jnp.float32)
    weighted = weighted + jnp.sum(
        ((2.0 * by_gradient * scaled)[None] * slopes)[:, :, None] * grads.astype(jnp.float32),
        axis=0,
    )
    weighted = weighted.astype(jnp.bfloat16)
    one_side = lax.dot_general(
        values, weighted, (((0,), (0,)), ((), ())), preferred_element_type=jnp.float32
    )
    return (point_density, one_side + one_side.T)


def band_product(left, right_padded):
    blocks = left.shape[0]
    total = None
    for offset_step in range(5):
        shifted = right_padded[offset_step : offset_step + blocks]
        widened = jnp.pad(shifted, ((0, 0), (2, 2), (0, 0), (0, 0)))
        picked = widened[:, 4 - offset_step : 9 - offset_step]
        term = jnp.einsum(
            "brk,bdkc->bdrc", left[:, offset_step], picked, preferred_element_type=jnp.float32
        )
        total = term if total is None else total + term
    return total


def window_of(band_three, lead, offset, functions):
    paired = lax.dynamic_slice_in_dim(band_three, lead, 2, 0)
    upper = jnp.concatenate([paired[0, 1], paired[0, 2]], axis=1)
    lower = jnp.concatenate([paired[1, 0], paired[1, 1]], axis=1)
    dense = jnp.concatenate([upper, lower], axis=0)
    return lax.dynamic_slice(dense, (offset, offset), (functions, functions))


def spread_term(summed, term, lead, offset):
    width = summed.shape[2]
    dense = lax.dynamic_update_slice(
        jnp.zeros((2 * width, 2 * width), summed.dtype), term, (offset, offset)
    )
    nothing = jnp.zeros((width, width), summed.dtype)
    upper = jnp.stack([nothing, dense[:width, :width], dense[:width, width:]])
    lower = jnp.stack([dense[width:, :width], dense[width:, width:], nothing])
    increment = jnp.stack([upper, lower])
    paired = lax.dynamic_slice_in_dim(summed, lead, 2, 0)
    return lax.dynamic_update_slice_in_dim(summed, paired + increment, lead, 0)


def times_current(left, current):
    near_right = padded(current, (("row", 0),), 2)
    return band_product(left, lax.all_gather(near_right, "col", axis=2, tiled=True))


def edge_rows(summed):
    blocks = summed.shape[0] - 2
    from_above = shifted_2(summed[0].astype(jnp.bfloat16), "row", -1).astype(jnp.float32)
    from_below = shifted_2(summed[blocks + 1].astype(jnp.bfloat16), "row", 1).astype(jnp.float32)
    own_rows = summed[1 : blocks + 1]
    return jnp.concatenate(
        [
            own_rows[:1] + from_below[None],
            own_rows[1 : blocks - 1],
            own_rows[blocks - 1 :] + from_above[None],
        ],
        axis=0,
    )


def by_gathers(density, pattern, windows, basis_values, basis_grads, weights):
    row_index = lax.axis_index("row")
    band_rows = density.shape[0]
    functions = basis_values.shape[2]
    step_size = functions // 3
    kept = (pattern > 0)[:, :, None, None]
    current = jnp.where(kept, density, jnp.zeros_like(density))
    for _ in range(ITERS):
        square = jnp.where(kept, times_current(current, current), 0.0).astype(jnp.bfloat16)
        cubic = times_current(square, current)
        current = jnp.where(kept, 3.0 * square.astype(jnp.float32) - 2.0 * cubic, 0.0).astype(
            jnp.bfloat16
        )
    rows_full = lax.all_gather(current, "col", axis=2, tiled=True)
    near_full = padded(rows_full, (("row", 0),), 1)
    near = near_full[:, 1:4]
    tiles_here = windows.shape[0]
    points = basis_values.shape[1]
    block_size = near.shape[2]

    def one_tile(tile_index, carry):
        summed, densities = carry
        position = tile_index.astype(jnp.int32)
        start_step = windows[position]
        lead = start_step // 2 - (band_rows * row_index - 1)
        offset = start_step % 2 * step_size
        window_block = window_of(near, lead, offset, functions)
        values = lax.dynamic_index_in_dim(basis_values, position, 0, keepdims=False)
        grads = lax.dynamic_index_in_dim(basis_grads, position, 1, keepdims=False)
        quadrature = lax.dynamic_index_in_dim(weights, position, 0, keepdims=False)
        point_density, contribution = tile_terms(values, grads, quadrature, window_block)
        summed = spread_term(summed, contribution, lead, offset)
        densities = lax.dynamic_update_index_in_dim(densities, point_density, position, 0)
        return (summed, densities)

    start_carry = (
        jnp.zeros((band_rows + 2, 3, block_size, block_size), jnp.float32),
        jnp.zeros((tiles_here, points), jnp.float32),
    )
    local_terms, densities = lax.fori_loop(0, tiles_here, one_tile, start_carry)
    owner_part = lax.psum_scatter(
        local_terms.astype(jnp.bfloat16), "col", scatter_dimension=2, tiled=True
    ).astype(jnp.float32)
    mine = edge_rows(owner_part)
    xc_matrix = jnp.where(kept, jnp.pad(mine, ((0, 0), (1, 1), (0, 0), (0, 0))), 0.0)
    return (current, xc_matrix, densities)


BF16 = jnp.bfloat16
F32 = jnp.float32


def mixed(index, turn, count):
    return index ^ turn if count & (count - 1) == 0 else (turn - index) % count


class Chain:
    def __init__(self, rows, cols):
        self.rows, self.cols, self.count = rows, cols, rows * cols

    def device(self, block_row):
        pair, step = divmod(block_row, 2 * self.cols)
        plane, core = divmod(step, 2)
        plane = plane if pair % 2 == 0 else self.cols - 1 - plane
        return (2 * pair + core) * self.cols + plane

    def step(self, row_index, col_index):
        pair, core = row_index // 2, row_index % 2
        plane = jnp.where(pair % 2 == 0, col_index, self.cols - 1 - col_index)
        return 2 * plane + core

    def to_rows(self, turn):
        pairs = []
        for row in range(self.rows):
            for col in range(self.cols):
                pairs.append((row * self.cols + col, self.device(row * self.cols + mixed(col, turn, self.cols))))
        return pairs

    def to_slices(self, turn):
        return [(b, a) for a, b in self.to_rows(turn)]

    def edges(self, turn):
        pairs, other = [], (turn + self.cols // 2) % self.cols
        for row in range(self.rows):
            if row + 1 < self.rows:
                pairs.append((self.device((row + 1) * self.cols - 1), (row + 1) * self.cols + turn))
            if row > 0:
                pairs.append((self.device(row * self.cols), (row - 1) * self.cols + other))
        return pairs

    def shift(self, by):
        return [(self.device(i), self.device(i + by)) for i in range(self.count) if 0 <= i + by < self.count]


SMALL = 12 << 20
LARGE = 60 << 20
BOTH = ("row", "col")
VMEM_SPEC = pl.BlockSpec(memory_space=pltpu.VMEM)
SMEM_SPEC = pl.BlockSpec(memory_space=pltpu.SMEM)


def with_ids(body, before):
    def wrapped(*refs):
        ids = [ref[0] for ref in refs[before : before + 3]]
        return body(*refs[:before], ids, *refs[before + 3 :])

    return wrapped


def small_call(body, scalars, arrays, outs, scratch=(), limit=SMALL):
    return pl.pallas_call(
        with_ids(body, len(scalars) - 3) if len(scalars) >= 3 else body,
        in_specs=[SMEM_SPEC] * len(scalars) + [VMEM_SPEC] * len(arrays),
        out_specs=[VMEM_SPEC] * len(outs),
        out_shape=[jax.ShapeDtypeStruct(s, d) for s, d in outs],
        scratch_shapes=[pltpu.VMEM(s, d) for s, d in scratch],
        compiler_params=pltpu.CompilerParams(vmem_limit_bytes=limit),
    )(*scalars, *arrays)


HELD = (0, 2, 3)
SENDS = ((1, 5), (2, 5), (0, 4), (0, 3))
NOTE = 16
PLACE, SLICE, BASE = range(3)


def grid_of(shape, axis):
    return lax.broadcasted_iota(jnp.int32, shape, axis)


def prepare(density, pattern, windows, ids):
    cols, _, high, block = density.shape
    tiles = windows.shape[0]

    def body(pattern_ref, windows_ref, ids, density_ref, *outs):
        row, lane = grid_of((NOTE, block), 0), grid_of((NOTE, block), 1)
        for turn in range(cols):
            j = mixed(ids[SLICE], turn, cols)
            for k, d in enumerate(HELD):
                value = density_ref[j, d]
                outs[turn][k * high : (k + 1) * high] = jnp.where(pattern_ref[j, d] > 0, value, jnp.zeros_like(value))
            note = jnp.zeros((NOTE, block), F32)
            for d in range(5):
                note = jnp.where((row == 0) & (lane == d), (pattern_ref[j, d] > 0).astype(F32), note)
            for tile in range(tiles):
                note = jnp.where((row == 1) & (lane == tile), (windows_ref[tile] - ids[BASE]).astype(F32), note)
            outs[turn][3 * high :] = note.astype(BF16)

    shapes = [((3 * high + NOTE, block), BF16)] * cols
    return small_call(body, [pattern, windows, *ids], [density], shapes, limit=LARGE)


def join_rows(pieces, place, block):
    cols = len(pieces)
    high = block // cols

    def body(ids, *refs):
        ins, (own, up, down, kept, steps) = refs[:cols], refs[cols:]
        row = grid_of((NOTE, block), 0)
        total = jnp.zeros((NOTE, block), F32)
        for turn in range(cols):
            source = mixed(ids[PLACE], turn, cols)
            at = pl.ds(pl.multiple_of(source * high, high), high)
            for k in range(3):
                value = ins[turn][k * high : (k + 1) * high]
                own[k, at] = value
                if k > 0:
                    up[k - 1, at] = value
                if k < 2:
                    down[k, at] = value
            note = ins[turn][3 * high :].astype(F32)
            total = jnp.where(row == source, note[1:2], total)
        kept[...] = note
        steps[...] = total.astype(BF16)

    two, three = ((2, block, block), BF16), ((3, block, block), BF16)
    shapes = [three, two, two, ((NOTE, block), F32), ((NOTE, block), BF16)]
    return small_call(body, place, pieces, shapes)


def exchange_rows(chain, sends):
    got = {}
    for by, send in zip((1, 2, -1, -2), sends):
        got[by] = lax.ppermute(send, BOTH, chain.shift(by))
    return got[1], got[2], got[-1], got[-2]


def purify_math(kept_ref, left, right, square, store):
    def product(left, d):
        far, total = d - 2, None
        for o in range(max(-2, far - 2), min(2, far + 2) + 1):
            term = jnp.dot(left(o), right(o, far), preferred_element_type=F32)
            total = term if total is None else total + term
        return jnp.where(kept_ref[0:1, d : d + 1] > 0.0, total, 0.0)

    for d in range(5):
        square[d] = product(left, d).astype(BF16)
    for d in range(5):
        value = 3.0 * square[d].astype(F32) - 2.0 * product(lambda o: square[o + 2], d)
        store(d, value.astype(BF16))


def purify_first(own, near, kept, block):
    places = [(a, b) for a in range(-2, 3) for b in range(-2, 3) if abs(a - b) <= 2]
    held = [(-2, -2), (-2, -1), (-1, -1), (-1, 0), (0, -2), (0, 0), (0, 1), (1, -1), (1, 1), (1, 2), (2, 0), (2, 2)]
    flipped = [(a, b) for a, b in places if (a, b) not in held]

    def body(kept_ref, own_ref, m1, m2, p1, p2, *refs):
        outs, (square, turned) = refs[:-2], refs[-2:]
        source = [(m2, 0), (m2, 1), (m1, 0), (m1, 1), (own_ref, 0), (own_ref, 1), (own_ref, 2)]
        source += [(p1, 0), (p1, 1), (p1, 2), (p2, 0), (p2, 1)]
        source = dict(zip(held, source))
        for k, (a, b) in enumerate(flipped):
            ref, at = source[b, a]
            turned[k] = ref[at].T
            source[a, b] = (turned, k)

        def block_at(a, b):
            ref, at = source[a, b]
            return ref[at]

        def store(d, value):
            outs[0][d] = value
            for out, (low, top) in zip(outs[1:], SENDS):
                if low <= d < top:
                    out[d - low] = value

        purify_math(kept_ref, lambda o: block_at(0, o), block_at, square, store)

    whole = ((5, block, block), BF16)
    shapes = [whole] + [((top - low, block, block), BF16) for low, top in SENDS]
    scratch = [whole, ((len(flipped), block, block), BF16)]
    return small_call(body, [], [kept, own] + list(near), shapes, scratch)


def purify_next(own, near, kept, block, place, steps, cols):
    high = block // cols
    last = place is not None

    def body(*refs):
        ids, refs = (refs[0], refs[1:]) if last else (None, refs)
        kept_ref, own_ref, m1, m2, p1, p2, steps_ref = refs[:7]
        outs, (square, whole_ref) = refs[7:-2], refs[-2:]

        def right(o, far):
            return (m2, m1, own_ref, p1, p2)[o + 2][far + (2, 2, 2, 1, 0)[o + 2]]

        def store(d, value):
            if last:
                whole_ref[d] = value
                return
            outs[0][d] = value
            for out, (low, top) in zip(outs[1:], SENDS):
                if low <= d < top:
                    out[d - low] = value

        purify_math(kept_ref, lambda o: own_ref[o + 2], right, square, store)
        if last:
            for turn in range(cols):
                at = pl.ds(pl.multiple_of(mixed(ids[PLACE], turn, cols) * high, high), high)
                for k in range(3):
                    outs[turn][k * high : (k + 1) * high] = whole_ref[k + 1, at]
                outs[turn][3 * high :] = steps_ref[...]
                for k in range(2):
                    outs[2 * cols + turn][k * high : (k + 1) * high] = whole_ref[4 * k, at]

                @pl.when(ids[PLACE] == cols - 1)
                def _():
                    outs[cols + turn][...] = whole_ref[2:4, high * turn : high * (turn + 1)]

                @pl.when(ids[PLACE] == 0)
                def _():
                    other = (turn + cols // 2) % cols
                    outs[cols + turn][...] = whole_ref[1:3, high * other : high * (other + 1)]

    whole = ((5, block, block), BF16)
    if last:
        shapes = [((3 * high + NOTE, block), BF16)] * cols + [((2, high, block), BF16)] * cols
        shapes += [((2 * high, block), BF16)] * cols
    else:
        shapes = [whole] + [((top - low, block, block), BF16) for low, top in SENDS]
    return small_call(body, place if last else [], [kept, own] + list(near) + [steps], shapes, [whole, whole])


def join_slices(pieces, far_pieces, ids, block, after):
    cols = len(pieces)
    high = block // cols

    def body(ids, *refs):
        near, far, out = refs[:cols], refs[cols : 2 * cols], refs[-1]
        for turn in range(cols):
            j = mixed(ids[SLICE], turn, cols)
            for k in range(3):
                out[j, k + 1] = near[turn][k * high : (k + 1) * high]
            for k in range(2):
                out[j, 4 * k] = far[turn][k * high : (k + 1) * high]

    return pl.pallas_call(
        with_ids(body, 0),
        in_specs=[SMEM_SPEC] * 3 + [VMEM_SPEC] * (2 * cols) + [pl.BlockSpec(memory_space=pl.ANY)],
        out_specs=VMEM_SPEC,
        out_shape=jax.ShapeDtypeStruct((cols, 5, high, block), BF16),
        compiler_params=pltpu.CompilerParams(vmem_limit_bytes=SMALL),
        name="join_slices",
    )(*ids, *pieces, *far_pieces, after)


def own_copy(windows):
    def body(windows_ref, out):
        for tile in range(windows.shape[0]):
            out[tile] = windows_ref[tile]

    return pl.pallas_call(
        body,
        in_specs=[SMEM_SPEC],
        out_specs=SMEM_SPEC,
        out_shape=jax.ShapeDtypeStruct(windows.shape, windows.dtype),
        compiler_params=pltpu.CompilerParams(vmem_limit_bytes=1 << 20),
    )(windows)


def read_steps(piece, cols, tiles):
    rows, block = piece.shape

    def body(piece_ref, steps):
        note = piece_ref[...].astype(F32)
        row, lane = grid_of((NOTE, block), 0), grid_of((NOTE, block), 1)
        for source in range(cols):
            for tile in range(tiles):
                here = jnp.where((row == source) & (lane == tile), note, 0.0)
                steps[source, tile] = jnp.sum(here).astype(jnp.int32)

    return pl.pallas_call(
        body,
        grid=(1,),
        in_specs=[pl.BlockSpec((NOTE, block), lambda i: (rows // NOTE - 1, 0))],
        out_specs=SMEM_SPEC,
        out_shape=jax.ShapeDtypeStruct((cols, tiles), jnp.int32),
        compiler_params=pltpu.CompilerParams(vmem_limit_bytes=1 << 20),
        name="read_steps",
    )(piece)


def slot_of(step, half):
    offset = step % 2
    first = (half - offset + 2) % 2
    return offset, first, (offset + first) // 2


def pack_windows(pieces, edges, steps, ids, block, tiles, functions):
    cols = len(pieces)
    high = block // cols
    part = functions // 3
    per_half = part // high

    def body(steps_ref, ids, *refs):
        ins, edge_ins, outs, near = refs[:cols], refs[cols : 2 * cols], refs[2 * cols : -1], refs[-1]
        here = ids[SLICE]
        for turn in range(cols):
            row = mixed(here, turn, cols) + 1
            for low in range(2):
                for b in range(2):
                    k = 1 - low + b
                    near[low, row, :, b * block : (b + 1) * block] = ins[turn][k * high : (k + 1) * high]

            @pl.when(here == turn)
            def _():
                for b in range(2):
                    near[0, 0, :, b * block : (b + 1) * block] = edge_ins[turn][b]

            @pl.when(here == (turn + cols // 2) % cols)
            def _():
                for b in range(2):
                    near[1, cols + 1, :, b * block : (b + 1) * block] = edge_ins[turn][b]

        half = here // per_half
        for to in range(cols):
            for tile in range(tiles):
                step = steps_ref[to, tile]
                offset, _, low = slot_of(step, half)
                lanes = pl.ds(pl.multiple_of(offset * part, part), functions)
                outs[tile][to, 0] = near[low, step // 2 + low, :, lanes]
                outs[tile][to, 1] = near[1, step // 2 + 1, :, lanes]

    return small_call(
        body, [steps, *ids], list(pieces) + list(edges),
        [((cols, 2, high, functions), BF16)] * tiles, [((2, cols + 2, high, 2 * block), BF16)],
    )


def pointwise(n, g, w, points):
    u = n * n + 1.0
    a = jnp.exp(jnp.log(u) * (2.0 / 3.0))
    ia = 1.0 / a
    t = (g[0] * g[0] + g[1] * g[1] + g[2] * g[2]) * (ia * ia)
    part = 1.0 / (1.0 + (mu_pbe / kappa_pbe) * t)
    enhance = 1.0 + kappa_pbe - kappa_pbe * part
    slope = mu_pbe * part * part
    by_gradient = -slater_cx * slope * ia
    by_density = -slater_cx * a * (n / u) * ((4.0 / 3.0) * enhance - (8.0 / 3.0) * t * slope)
    scaled = w * (1.0 / points)
    return 0.5 * by_density * scaled, [2.0 * by_gradient * scaled * gk for gk in g]


def tile_call(tile, basis_values, basis_grads, weights, pieces, windows, ids, rows=1024, parts=2):
    tiles, points, functions = basis_values.shape
    cols, _, high, _ = pieces.shape
    part = functions // 3
    per_half = part // high
    count, sub, lanes = points // rows, rows // parts, functions // 128

    def body(windows_ref, ids, v_ref, g_ref, w_ref, pieces_ref, dens_ref, term_ref, win_ref, kept_ref, y_ref, *bufs):
        i = pl.program_id(0)
        step = windows_ref[tile] - ids[BASE]
        offset = step % 2
        x_refs, z_refs = bufs[:parts], bufs[parts:]
        ones = jnp.ones((8, 128), BF16)

        @pl.when(i == 0)
        def _():
            kept_ref[...] = jnp.zeros(kept_ref.shape, BF16)
            z_refs[-1][...] = jnp.zeros(z_refs[-1].shape, BF16)
            y_ref[...] = jnp.zeros(y_ref.shape, F32)
            for h in range(3):
                for s in range(per_half):
                    source = per_half * ((offset + h) % 2) + s
                    win_ref[part * h + high * s : part * h + high * (s + 1)] = pieces_ref[source, h // 2]

        def columns(x):
            return [x[:, 128 * j : 128 * (j + 1)] for j in range(lanes)]

        def project(k):
            v = v_ref[sub * k : sub * (k + 1)]
            x_refs[k][...] = jnp.dot(v, win_ref[...], preferred_element_type=F32).astype(BF16)

        def row_sums(k):
            at = slice(sub * k, sub * (k + 1))
            x = columns(x_refs[k][...])

            def total(a):
                partial = sum(p * q for p, q in zip(x, columns(a)))
                return lax.dot_general(ones, partial, (((1,), (1,)), ((), ())), preferred_element_type=F32)

            return [total(v_ref[at])] + [total(g_ref[q, at]) for q in range(3)]

        def back(k):
            v = kept_ref[...] if k < 0 else v_ref[sub * k : sub * (k + 1)]
            y_ref[...] += lax.dot_general(
                v, z_refs[k][...], (((0,), (0,)), ((), ())), preferred_element_type=F32
            )

        def weigh(k, sums):
            at = slice(sub * k, sub * (k + 1))
            n = sums[0] * (1.0 / functions)
            g = [q * (2.0 / functions) for q in sums[1:]]
            dens_ref[:, at] = n[0:1]
            c0, ck = pointwise(n, g, jnp.broadcast_to(w_ref[tile : tile + 1, at], (8, sub)), points)
            factors = [c.astype(BF16) for c in [c0] + ck]
            for b in range(sub // 128):
                r = slice(sub * k + 128 * b, sub * k + 128 * (b + 1))
                f = [jnp.concatenate([c[:, 128 * b : 128 * (b + 1)]] * 16, axis=0).T for c in factors]
                arrays = [v_ref[r]] + [g_ref[q, r] for q in range(3)]
                for j in range(lanes):
                    t = [u * a[:, 128 * j : 128 * (j + 1)] for u, a in zip(f, arrays)]
                    z_refs[k][128 * b : 128 * (b + 1), 128 * j : 128 * (j + 1)] = (t[0] + t[1]) + (t[2] + t[3])

        project(0)
        for k in range(parts):
            if k + 1 < parts:
                project(k + 1)
            sums = row_sums(k)
            back(k - 1)
            weigh(k, sums)
        kept_ref[...] = v_ref[sub * (parts - 1) :]

        @pl.when(i == count - 1)
        def _():
            back(-1)
            y = y_ref[...]
            y_ref[...] = y + y.T
            for to in range(cols):
                _, first, _ = slot_of(step, to // per_half)
                start = pl.multiple_of(part * first + high * (to % per_half), high)
                term_ref[to, 0] = y_ref[pl.ds(start, high)].astype(BF16)
                start = 2 * part + high * (to % per_half)
                term_ref[to, 1] = y_ref[start : start + high].astype(BF16)

    return pl.pallas_call(
        with_ids(body, 1),
        grid=(count,),
        in_specs=[
            SMEM_SPEC,
            SMEM_SPEC,
            SMEM_SPEC,
            SMEM_SPEC,
            pl.BlockSpec((None, rows, functions), lambda i: (tile, i, 0)),
            pl.BlockSpec((3, None, rows, functions), lambda i: (0, tile, i, 0)),
            pl.BlockSpec((tiles, rows), lambda i: (0, i)),
            VMEM_SPEC,
        ],
        out_specs=[pl.BlockSpec((1, rows), lambda i: (0, i)), VMEM_SPEC],
        out_shape=[
            jax.ShapeDtypeStruct((1, points), F32),
            jax.ShapeDtypeStruct(pieces.shape, BF16),
        ],
        scratch_shapes=[
            pltpu.VMEM((functions, functions), BF16),
            pltpu.VMEM((sub, functions), BF16),
            pltpu.VMEM((functions, functions), F32),
        ]
        + [pltpu.VMEM((sub, functions), BF16)] * (2 * parts),
        compiler_params=pltpu.CompilerParams(vmem_limit_bytes=48 << 20),
        name="tile",
    )(windows, *ids, basis_values, basis_grads, weights, pieces)


def add_terms(terms, steps, place, block):
    tiles = len(terms)
    cols, _, high, functions = terms[0].shape
    part = functions // 3
    per_half = part // high

    def body(steps_ref, ids, *refs):
        ins, (own, to_above, to_below, total) = refs[:tiles], refs[tiles:]
        total[...] = jnp.zeros(total.shape, F32)
        half = ids[SLICE] // per_half
        for source in range(cols):
            for tile in range(tiles):
                step = steps_ref[source, tile]
                offset, first, low = slot_of(step, half)
                lanes = pl.ds(pl.multiple_of(offset * part, part), functions)
                total[low, step // 2 + low, :, lanes] += ins[tile][source, 0].astype(F32)

                @pl.when(first == 0)
                def _():
                    total[1, step // 2 + 1, :, lanes] += ins[tile][source, 1].astype(F32)

        for row in range(1, cols + 1):
            own[row - 1, 0] = total[1, row, :, :block]
            own[row - 1, 1] = total[1, row, :, block:] + total[0, row, :, :block]
            own[row - 1, 2] = total[0, row, :, block:]
        for b in range(2):
            at = slice(b * block, (b + 1) * block)
            to_above[b] = total[0, 0, :, at].astype(BF16)
            to_below[b] = total[1, cols + 1, :, at].astype(BF16)

    edge = ((2, high, block), BF16)
    return small_call(
        body, [steps, *place], list(terms),
        [((cols, 3, high, block), F32), edge, edge], [((2, cols + 2, high, 2 * block), F32)],
    )


def by_block_rows(density, pattern, windows, basis_values, basis_grads, weights):
    rows, cols = lax.axis_size("row"), lax.axis_size("col")
    row_index, col_index = lax.axis_index("row"), lax.axis_index("col")
    block = density.shape[3]
    tiles, _, functions = basis_values.shape
    chain = Chain(rows, cols)
    place = chain.step(row_index, col_index) % cols
    ids = [x.astype(jnp.int32).reshape(1) for x in (place, col_index, 2 * cols * row_index - 2)]
    pieces = prepare(density, pattern, windows, ids)
    pieces = [lax.ppermute(p, BOTH, chain.to_rows(turn)) for turn, p in enumerate(pieces)]
    own, up, down, kept_row, steps = join_rows(pieces, ids, block)
    sends = (up, up, own, down)
    for iteration in range(ITERS):
        near = exchange_rows(chain, sends)
        if iteration == 0:
            out = purify_first(own, near, kept_row, block)
        else:
            out = purify_next(own, near, kept_row, block, ids if iteration == ITERS - 1 else None, steps, cols)
        own, sends = out[0], out[1:]
    pieces, edges = [], []
    for turn in range(cols):
        pieces.append(lax.ppermute(out[turn], BOTH, chain.to_slices(turn)))
    for turn in range(cols):
        edges.append(lax.ppermute(out[cols + turn], BOTH, chain.edges(turn)))
    steps = read_steps(pieces[0], cols, tiles)
    sent = pack_windows(pieces, edges, steps, ids, block, tiles, functions)
    far_pieces = []
    for turn in range(cols):
        far_pieces.append(lax.ppermute(out[2 * cols + turn], BOTH, chain.to_slices(turn)))

    windows = own_copy(windows)
    densities, terms = [], []
    for tile in range(tiles):
        window = lax.all_to_all(sent[tile], "col", 0, 0, tiled=True)
        dens, term = tile_call(tile, basis_values, basis_grads, weights, window, windows, ids)
        densities.append(dens)
        terms.append(lax.all_to_all(term, "col", 0, 0, tiled=True))
    purified = join_slices(pieces, far_pieces, ids, block, term)
    mine, to_above, to_below = add_terms(terms, steps, ids, block)
    from_below = shifted_2(to_above, "row", -1).astype(F32)
    from_above = shifted_2(to_below, "row", 1).astype(F32)
    first = jnp.pad(from_above[None], ((0, cols - 1), (0, 1), (0, 0), (0, 0)))
    last = jnp.pad(from_below[None], ((cols - 1, 0), (1, 0), (0, 0), (0, 0)))
    summed = jnp.pad(mine + first + last, ((0, 0), (1, 1), (0, 0), (0, 0)))
    xc_matrix = jnp.where((pattern > 0)[:, :, None, None], summed, 0.0)
    return purified, xc_matrix, jnp.concatenate(densities)


def on_device(density, pattern, windows, basis_values, basis_grads, weights):
    rows, cols = lax.axis_size("row"), lax.axis_size("col")
    band_rows, block, functions = density.shape[0], density.shape[3], basis_values.shape[2]
    fits = (
        band_rows == cols
        and rows % 2 == 0
        and cols > 1
        and 2 * functions == 3 * block
        and functions // 3 % density.shape[2] == 0
        and cols <= NOTE
        and density.shape[2] % NOTE == 0
        and 2 * cols + 2 <= 256
        and basis_values.shape[1] % 1024 == 0
    )
    plan = by_block_rows if fits else by_gathers
    return plan(density, pattern, windows, basis_values, basis_grads, weights)


def solution(mesh):
    placed = (
        P("row", None, "col", None),
        P("row", None),
        P(("row", "col")),
        P(("row", "col"), None, None),
        P(None, ("row", "col"), None, None),
        P(("row", "col"), None),
    )
    return jax.shard_map(
        on_device,
        mesh=mesh,
        in_specs=placed,
        out_specs=(
            P("row", None, "col", None),
            P("row", None, "col", None),
            P(("row", "col"), None),
        ),
        check_vma=False,
    )
```
